32 devices in a mesh: depth: 4 (over y, x), res: 8 (over z, core).
Axes of the slice: x: 2, y: 2, z: 4, core: 2. Of those that a mesh axis runs over, the one named last changes fastest.
Arguments:
- alignment_left: bfloat16 [1024, 8192], P('depth', 'res'), may hold values from -6 to 6
- alignment_right: bfloat16 [1024, 8192], P('depth', 'res'), may hold values from -6 to 6
- window_starts: int32 [4], replicated, may hold values from 0 to 248
- outer_product_weight: bfloat16 [1024, 128], replicated, may hold values from -6 to 6
- outer_product_bias: float32 [128], replicated, may hold values from -3 to 3
- query_key_value_gate_weight: bfloat16 [128, 512], replicated, may hold values from -0.5 to 0.5
- output_weight: bfloat16 [128, 128], replicated, may hold values from -2 to 2
- triangle_pair_bias: bfloat16 [4, 256, 256], P(None, 'res'), may hold values from -3 to 260
- residue_chain: int32 [256], replicated, may hold values from 0 to 7, never falling along the last dimension, each value on 1 to 64 neighbouring positions
- interchain_offset: float32 [4], replicated, may hold values from -3 to -0.5
Outputs:
- pair_strip: bfloat16 [32, 256, 128], P('depth', 'res')
- update: bfloat16 [32, 256, 128], P('depth', 'res')
The draws below stay inside these ranges and needn't reach their ends.
All inputs are finite; a program needn't handle non-finite values.
Results may differ from the reference program's by a relative error of at most 0.014.
Values may be sent and summed in bfloat16 or wider, within the bound.
No kernel may reach another device: no remote copies, remote signals or barrier semaphores. Data moves between devices by JAX's collectives and lax.ppermute only.
A program may use at most 128 MiB of HBM per device.

```python
import math
import jax
import jax.numpy as jnp
import numpy as np
from jax import lax

PROJ_CHANNELS = 32
CZ = 128
H = 4
DH = 32
R_DEV = 8
SEQUENCE_COUNT = 1024
RESIDUE_COUNT = 256
GROUPS = 4
R = 32


def draw_triangle_pair_bias(key, part):
    base_key = jax.random.fold_in(key, 11)
    row_key = jax.random.fold_in(key, 12)
    level_key = jax.random.fold_in(key, 13)
    first_key = jax.random.fold_in(key, 14)
    second_key = jax.random.fold_in(key, 15)
    forced_key = jax.random.fold_in(key, 16)
    background = jnp.clip(jax.random.normal(base_key, (H, RESIDUE_COUNT, RESIDUE_COUNT), jnp.float32), -3.0, 3.0)
    forced_row = jax.random.randint(forced_key, (), 0, RESIDUE_COUNT)
    forced = (jnp.arange(H)[:, None] == 0) & (jnp.arange(RESIDUE_COUNT)[None, :] == forced_row)
    chosen = (jax.random.randint(row_key, (H, RESIDUE_COUNT), 0, 64) == 0) | forced
    levels = jnp.array([110.0, 180.0, 260.0], jnp.float32)
    level_row = levels[jax.random.randint(level_key, (H, RESIDUE_COUNT), 0, 3)]
    level_row = jnp.where(forced, 260.0, level_row)
    first_col = jax.random.randint(first_key, (H, RESIDUE_COUNT), 0, RESIDUE_COUNT)
    second = (first_col + jax.random.randint(second_key, (H, RESIDUE_COUNT), 1, RESIDUE_COUNT)) % RESIDUE_COUNT
    column = jnp.arange(RESIDUE_COUNT)[None, None, :]
    peaked = jnp.where(column == first_col[:, :, None], level_row[:, :, None], jnp.where(column == second[:, :, None], level_row[:, :, None] - 2.0, background))
    return jnp.where(chosen[:, :, None], peaked, background).astype(jnp.bfloat16)


def set_ends(entries, rng, smallest, top_value):
    spot = [jax.random.randint(jax.random.fold_in(rng, axis), (), 0, length) for axis, length in enumerate(entries.shape)]
    widest = entries.shape.index(max(entries.shape))
    next_to = spot[:widest] + [(spot[widest] + 1) % entries.shape[widest]] + spot[widest + 1:]
    return entries.at[tuple(spot)].set(smallest).at[tuple(next_to)].set(top_value)


def level_of(key, dims, pieces, least, largest):
    def one(axis_at, shards_of):
        draws = jax.random.uniform(jax.random.fold_in(jax.random.fold_in(key, 6), axis_at), (shards_of,), jnp.float32, least / len(pieces), largest / len(pieces))
        return jnp.repeat(jnp.exp(draws), dims[axis_at] // shards_of).reshape((-1,) + (1,) * (len(dims) - axis_at - 1))

    factor_of = one(*pieces[0])
    for cut in pieces[1:]:
        factor_of = factor_of * one(*cut)
    return factor_of


def split_up(amount, total, most, skew):
    weights = [(1 << 20) // math.isqrt(grade ** skew) + 1 for grade in range(2, amount + 1)]
    spare, given = total - most - (amount - 1), [1] * (amount - 1)
    while spare > 0:
        movable = [i for i in range(amount - 1) if given[i] < most]
        pool, remaining = sum([weights[i] for i in movable]), spare
        for i in movable:
            extra = min(most - given[i], max(1, remaining * weights[i] // pool), spare)
            given[i] = given[i] + extra
            spare = spare - extra
    return np.array([most] + given)


def uneven(rng, amount, total, bound, lean):
    if amount == 2:
        one = jax.random.randint(rng, (), max(1, total - bound), min(bound, total - 1) + 1)
        return jnp.stack([one, total - one])
    sizes = jnp.asarray(split_up(amount, total, bound, lean), jnp.int32)
    couples = (amount - 1) // 2
    giver, taker = sizes[1:1 + 2 * couples:2], sizes[2:2 + 2 * couples:2]
    room = jnp.minimum(giver - 1, bound - taker)
    moved = jax.random.randint(jax.random.fold_in(rng, 1), (couples,), 0, 1 << 20) % (room + 1)
    sizes = sizes.at[1:1 + 2 * couples:2].set(giver - moved).at[2:2 + 2 * couples:2].set(taker + moved)
    return sizes[jax.random.permutation(jax.random.fold_in(rng, 2), amount)]


def noise(key, extent, spread, reach, shards=(), kind=jnp.bfloat16):
    values = jax.random.normal(key, extent, jnp.float32) * spread
    if len(shards) > 0:
        values = level_of(key, extent, shards, -0.22, 0.18) * values
    return jnp.clip(values, min=-reach, max=reach).astype(kind)


def setup_inputs(seed: int = 0) -> dict:
    seeds = jax.random.split(jax.random.key(seed), 11)
    alignment_left = noise(seeds[0], (SEQUENCE_COUNT, RESIDUE_COUNT * PROJ_CHANNELS), 1.0, 6.0, ((0, 4), (1, 8)))
    alignment_right = noise(seeds[1], (SEQUENCE_COUNT, RESIDUE_COUNT * PROJ_CHANNELS), 1.0, 6.0, ((0, 4), (1, 8)))
    window_starts = set_ends(jax.random.randint(seeds[2], (GROUPS,), 0, RESIDUE_COUNT - R_DEV + 1), jax.random.fold_in(seeds[2], 1), 0, RESIDUE_COUNT - R_DEV).astype(jnp.int32)
    outer_product_weight = noise(seeds[3], (PROJ_CHANNELS * PROJ_CHANNELS, CZ), (0.03 * SEQUENCE_COUNT ** 0.5), 6.0)
    outer_product_bias = noise(seeds[4], (CZ,), 0.5, 3.0, (), jnp.float32)
    query_key_value_gate_weight = noise(seeds[5], (CZ, 4 * CZ), CZ ** -0.5, 0.5)
    output_weight = noise(seeds[6], (CZ, CZ), (CZ // 16) ** -0.5, 2.0)
    triangle_pair_bias = draw_triangle_pair_bias(jax.random.fold_in(seeds[10], 71), 0)
    residue_chain = jnp.searchsorted(jnp.cumsum(uneven(seeds[8], 8, RESIDUE_COUNT, RESIDUE_COUNT // 4, 1)), jnp.arange(RESIDUE_COUNT), side="right").astype(jnp.int32)
    interchain_offset = jnp.clip(jax.random.uniform(seeds[9], (H,), jnp.float32, -3.0, -0.5), -3.0, -0.5)
    return dict(alignment_left=alignment_left, alignment_right=alignment_right, window_starts=window_starts, outer_product_weight=outer_product_weight, outer_product_bias=outer_product_bias, query_key_value_gate_weight=query_key_value_gate_weight, output_weight=output_weight, triangle_pair_bias=triangle_pair_bias, residue_chain=residue_chain, interchain_offset=interchain_offset)


epsilon = 1e-05

def layer_norm(values):
    average = lax.optimization_barrier(jnp.mean(values, axis=-1, keepdims=True))
    centred = values - average
    variance = lax.optimization_barrier(jnp.mean(centred * centred, axis=-1, keepdims=True))
    return centred * lax.rsqrt(variance + epsilon)

def reference(alignment_left, alignment_right, window_starts, outer_product_weight, outer_product_bias, query_key_value_gate_weight, output_weight, triangle_pair_bias, residue_chain, interchain_offset):
    gathered_left = alignment_left.reshape(SEQUENCE_COUNT, RESIDUE_COUNT, PROJ_CHANNELS)
    gathered_right = alignment_right.reshape(SEQUENCE_COUNT, RESIDUE_COUNT, PROJ_CHANNELS).astype(jnp.float32)
    row_ids = (window_starts[:, None] + jnp.arange(R_DEV, dtype=jnp.int32)[None, :]).astype(jnp.int32)
    weight = outer_product_weight.astype(jnp.float32)

    def outer_block(block_rows):
        picked = jnp.take(gathered_left, block_rows, axis=1).astype(jnp.float32)
        outer_prod = jnp.einsum('hbv,hqz->bqvz', picked, gathered_right, precision=lax.Precision.HIGHEST)
        flat_outer = outer_prod.reshape(R_DEV * RESIDUE_COUNT, PROJ_CHANNELS * PROJ_CHANNELS)
        projected = jnp.dot(flat_outer, weight, precision=lax.Precision.HIGHEST)
        return (projected / SEQUENCE_COUNT + outer_product_bias[None, :]).astype(jnp.bfloat16).reshape(R_DEV, RESIDUE_COUNT, CZ)
    pair_strip = lax.map(outer_block, row_ids).reshape(R, RESIDUE_COUNT, CZ)
    differ = (residue_chain[:, None] != residue_chain[None, :]).astype(jnp.float32)
    full_bias = triangle_pair_bias.astype(jnp.float32) + interchain_offset[:, None, None] * differ[None, :, :]
    score_scale = DH ** (-0.5)

    def attend_row(pair_row):
        normed = layer_norm(pair_row.astype(jnp.float32)).astype(jnp.bfloat16)
        projection = jnp.dot(normed, query_key_value_gate_weight, preferred_element_type=jnp.float32).astype(jnp.bfloat16)
        queries = projection[:, :CZ].reshape(RESIDUE_COUNT, H, DH).astype(jnp.float32)
        key_heads = projection[:, CZ:2 * CZ].reshape(RESIDUE_COUNT, H, DH).astype(jnp.float32)
        value_heads = projection[:, 2 * CZ:3 * CZ].reshape(RESIDUE_COUNT, H, DH).astype(jnp.float32)
        gate_pre = projection[:, 3 * CZ:].astype(jnp.float32)
        scores = jnp.einsum('qhd,khd->hqk', queries, key_heads, precision=lax.Precision.HIGHEST) * score_scale + full_bias
        row_max = lax.optimization_barrier(jnp.max(scores, axis=-1, keepdims=True))
        weights = jnp.exp(scores - row_max)
        denom = lax.optimization_barrier(jnp.sum(weights, axis=-1))
        rounded = lax.optimization_barrier(weights.astype(jnp.bfloat16)).astype(jnp.float32)
        attended = jnp.einsum('hqk,khd->qhd', rounded, value_heads, precision=lax.Precision.HIGHEST)
        attended = attended / jnp.transpose(denom)[:, :, None]
        gated_out = (jax.nn.sigmoid(gate_pre) * attended.reshape(RESIDUE_COUNT, CZ)).astype(jnp.bfloat16)
        return jnp.dot(gated_out, output_weight, preferred_element_type=jnp.float32).astype(jnp.bfloat16)
    update = lax.map(attend_row, pair_strip)
    return (pair_strip, update)
```

```python
import functools

import jax
import jax.numpy as jnp
from jax import lax
from jax.experimental import pallas as pl
from jax.experimental.pallas import tpu as pltpu
from jax.sharding import PartitionSpec as P

PROJ_CHANNELS = 32
CZ = 128
H = 4
DH = 32
R_DEV = 8
LANES = 128
PACK = LANES // PROJ_CHANNELS
WINDOW = R_DEV * PROJ_CHANNELS
SPAN = WINDOW + LANES

epsilon = 1e-05
VMEM = pl.BlockSpec(memory_space=pltpu.VMEM)
SMEM = pl.BlockSpec(memory_space=pltpu.SMEM)
BF = jnp.bfloat16
F32 = jnp.float32


def call(kernel, outs, specs, scratch=(), flops=0, name=None):
    return pl.pallas_call(
        kernel,
        out_shape=outs,
        in_specs=specs,
        out_specs=jax.tree.map(lambda _: VMEM, outs),
        scratch_shapes=list(scratch),
        name=name,
        cost_estimate=pl.CostEstimate(
            flops=flops, bytes_accessed=1 << 20, transcendentals=0
        ),
    )


def prep_kernel(idx, off, w_ref, tri_ref, chain_ref, wbd_ref, bias_ref):
    wbd_ref[...] = jnp.zeros_like(wbd_ref)
    for c in range(PROJ_CHANNELS):
        block = w_ref[c * PROJ_CHANNELS : (c + 1) * PROJ_CHANNELS, :]
        for j in range(PACK):
            row = c * LANES + j * PROJ_CHANNELS
            wbd_ref[row : row + PROJ_CHANNELS, j * CZ : (j + 1) * CZ] = block
    tokens, keys = tri_ref.shape[1:]
    first = idx[1] * tokens
    chain = jnp.broadcast_to(chain_ref[...], (tokens, keys))
    rows = lax.broadcasted_iota(jnp.int32, (tokens, keys), 0)
    cols = lax.broadcasted_iota(jnp.int32, (tokens, keys), 1)
    own = jnp.sum(jnp.where(cols == rows + first, chain, 0), axis=1, keepdims=True)
    differ = (chain != own).astype(F32)
    for h in range(H):
        bias_ref[h * tokens : (h + 1) * tokens, :] = (
            tri_ref[h].astype(F32) + off[h] * differ
        )


def select_kernel(idx, starts, own_ref, recv_ref, out_ref, chip_ref):
    chips, size, half = out_ref.shape
    width = own_ref.shape[1]
    res = idx[1]
    core = res % 2
    z = res // 2
    own_at = pl.multiple_of(core * width, LANES)
    recv_at = pl.multiple_of((1 - core) * width, LANES)
    seq_at = pl.multiple_of(core * half, half)
    chip_ref[:, pl.ds(own_at, width)] = own_ref[pl.ds(seq_at, half), :]
    chip_ref[:, pl.ds(recv_at, width)] = recv_ref[...]
    m = lax.broadcasted_iota(jnp.int32, (size, SPAN), 0)
    lane = lax.broadcasted_iota(jnp.int32, (size, SPAN), 1)
    delta = lane - (m % R_DEV) * PROJ_CHANNELS - m // R_DEV
    for k in range(chips):
        g = jnp.bitwise_xor(z, k)
        split = WINDOW // size
        first = g % split * (size // R_DEV)
        start = starts[g // split] * PROJ_CHANNELS - z * (2 * width)
        base = jnp.clip(start, 0, 2 * width - SPAN) // LANES * LANES
        base = pl.multiple_of(base, LANES)
        pick = (delta == start + first - base).astype(F32).astype(BF)
        out_ref[k] = lax.dot_general(
            pick,
            chip_ref[:, pl.ds(base, SPAN)],
            (((1,), (1,)), ((), ())),
            preferred_element_type=F32,
        ).astype(BF)


def outer_kernel(chips, idx, *refs):
    mine = refs[:chips]
    theirs, b_ref, wbd_ref, out_ref, at_ref, lhs_ref, acc_ref = refs[chips:]
    size, half = mine[0].shape
    groups = out_ref.shape[0]
    z = idx[1] // 2
    core = idx[1] % 2
    mine_at = pl.multiple_of(core * half, LANES)
    theirs_at = pl.multiple_of((1 - core) * half, LANES)
    for k in range(chips):
        row = pl.multiple_of(jnp.bitwise_xor(z, k) * size, size)
        at_ref[pl.ds(row, size), pl.ds(mine_at, half)] = mine[k][...]
        at_ref[pl.ds(row, size), pl.ds(theirs_at, half)] = theirs[k]
    width = b_ref.shape[1]
    rows = groups * R_DEV
    for n in range(width // (2 * LANES)):
        part = jnp.dot(
            at_ref[...],
            b_ref[:, n * 2 * LANES : (n + 1) * 2 * LANES],
            preferred_element_type=F32,
        ).reshape(groups, PROJ_CHANNELS, R_DEV, 2 * LANES)
        for c in range(PROJ_CHANNELS):
            for q in range(2):
                slab = part[:, c, :, q * LANES : (q + 1) * LANES].reshape(rows, LANES)
                lhs_ref[
                    (2 * n + q) * rows : (2 * n + q + 1) * rows,
                    c * LANES : (c + 1) * LANES,
                ] = slab.astype(BF)
    acc = jnp.dot(lhs_ref[...], wbd_ref[...], preferred_element_type=F32)
    chunks = width // LANES
    acc_ref[...] = acc.reshape(chunks, groups, R_DEV, PACK * CZ)
    for k in range(groups):
        g = jnp.bitwise_xor(idx[0], k)
        block = acc_ref[:, g]
        block = jnp.stack(
            [block[:, :, j * CZ : (j + 1) * CZ] for j in range(PACK)], axis=1
        )
        out_ref[k] = block.reshape(chunks * PACK * R_DEV, CZ).astype(BF)


def norm_kernel(scale, *refs):
    parts = refs[:-4]
    bias_ref, pair_ref, normed_ref, sum_ref = refs[-4:]
    total = parts[0][...].astype(F32)
    for p in parts[1:]:
        total = total + p[...].astype(F32)
    sum_ref[...] = total * scale + bias_ref[...]
    tokens = pair_ref.shape[1]
    for u in range(R_DEV):
        pair = sum_ref[pl.ds(u, tokens, stride=R_DEV), :].astype(BF)
        pair_ref[u] = pair
        values = pair.astype(F32)
        centred = values - jnp.mean(values, axis=-1, keepdims=True)
        variance = jnp.mean(centred * centred, axis=-1, keepdims=True)
        normed_ref[u] = (centred * lax.rsqrt(variance + epsilon)).astype(BF)


def query_kernel(normed_ref, w_ref, q_ref, gate_ref):
    rows = R_DEV * normed_ref.shape[1]
    x = normed_ref[...].reshape(rows, CZ)
    q_ref[...] = jnp.dot(x, w_ref[:, :CZ], preferred_element_type=F32).astype(BF)
    g = jnp.dot(x, w_ref[:, 3 * CZ :], preferred_element_type=F32).astype(BF)
    gate_ref[...] = jax.nn.sigmoid(g.astype(F32))


def attend_kernel(chips, idx, *refs):
    mine = refs[:chips]
    theirs, q_ref, gate_ref, w_ref, wo_ref, bias_ref, out_ref, all_ref, gated_ref = refs[chips:]
    tokens = mine[0].shape[1]
    z = idx[1] // 2
    core = idx[1] % 2
    for k in range(chips):
        chip = jnp.bitwise_xor(z, k) * 2
        mine_at = pl.multiple_of((chip + core) * tokens, tokens)
        theirs_at = pl.multiple_of((chip + 1 - core) * tokens, tokens)
        all_ref[:, pl.ds(mine_at, tokens), :] = mine[k][...]
        all_ref[:, pl.ds(theirs_at, tokens), :] = theirs[k]
    scale = DH ** (-0.5)
    lane_head = lax.broadcasted_iota(jnp.int32, (tokens, CZ), 1) // DH
    for u in range(R_DEV):
        kv = jnp.dot(
            all_ref[u], w_ref[:, CZ : 3 * CZ], preferred_element_type=F32
        ).astype(BF)
        q = q_ref[u * tokens : (u + 1) * tokens, :]
        spread = jnp.concatenate(
            [jnp.where(lane_head == h, q, jnp.zeros_like(q)) for h in range(H)], axis=0
        )
        scores = lax.dot_general(
            spread, kv[:, :CZ], (((1,), (1,)), ((), ())), preferred_element_type=F32
        )
        scores = scores * scale + bias_ref[...]
        weights = jnp.exp(scores - jnp.max(scores, axis=-1, keepdims=True))
        denom = jnp.sum(weights, axis=-1, keepdims=True)
        value = jnp.dot(weights.astype(BF), kv[:, CZ:], preferred_element_type=F32)
        value = value / denom
        attended = jnp.zeros((tokens, CZ), F32)
        for h in range(H):
            attended = jnp.where(
                lane_head == h, value[h * tokens : (h + 1) * tokens, :], attended
            )
        gated_ref[u * tokens : (u + 1) * tokens, :] = (
            gate_ref[u * tokens : (u + 1) * tokens, :] * attended
        ).astype(BF)
    out = jnp.dot(gated_ref[...], wo_ref[...], preferred_element_type=F32)
    out_ref[...] = out.astype(BF).reshape(R_DEV, tokens, CZ)


def swap(x, axis, mask):
    n = lax.axis_size(axis)
    return lax.ppermute(x, axis, [(i, i ^ mask) for i in range(n)])


def body(
    alignment_left,
    alignment_right,
    window_starts,
    outer_product_weight,
    outer_product_bias,
    query_key_value_gate_weight,
    output_weight,
    triangle_pair_bias,
    residue_chain,
    interchain_offset,
):
    depth_count = lax.axis_size("depth")
    res_count = lax.axis_size("res")
    groups = window_starts.shape[0]
    chips = res_count // 2
    size = groups * WINDOW // chips
    assert groups == depth_count and WINDOW % size == 0
    seqs, width = alignment_left.shape
    half = seqs // 2
    tokens = width // PROJ_CHANNELS
    keys = residue_chain.shape[0]
    rows = groups * R_DEV
    res = lax.axis_index("res")
    idx = jnp.stack([lax.axis_index("depth"), res]).astype(jnp.int32)

    core = res % 2
    sent = lax.dynamic_slice_in_dim(alignment_left, (1 - core) * half, half, 0)
    recv = swap(sent, "res", 1)

    wbd, bias = call(
        prep_kernel,
        (
            jax.ShapeDtypeStruct((PROJ_CHANNELS * LANES, PACK * CZ), BF),
            jax.ShapeDtypeStruct((H * tokens, keys), F32),
        ),
        [SMEM, SMEM, VMEM, VMEM, VMEM],
        flops=1 << 28,
        name="prep",
    )(idx, interchain_offset, outer_product_weight, triangle_pair_bias, residue_chain[None, :])

    picked = call(
        select_kernel,
        jax.ShapeDtypeStruct((chips, size, half), BF),
        [SMEM, SMEM, VMEM, VMEM],
        [pltpu.VMEM((half, 2 * width), BF)],
        flops=1 << 28,
        name="select",
    )(idx, window_starts, alignment_left, recv)
    piece = picked[0]
    for k in range(1, chips):
        piece = piece + swap(picked[k], "res", 2 * k)
    mine = [piece] + [swap(piece, "res", 2 * k) for k in range(1, chips)]
    theirs = swap(jnp.stack(mine), "res", 1)

    partial = call(
        functools.partial(outer_kernel, chips),
        jax.ShapeDtypeStruct((groups, R_DEV * tokens, CZ), BF),
        [SMEM] + [VMEM] * (chips + 3),
        [
            pltpu.VMEM((groups * WINDOW, seqs), BF),
            pltpu.VMEM((rows * width // LANES, PROJ_CHANNELS * LANES), BF),
            pltpu.VMEM((width // LANES, groups, R_DEV, PACK * CZ), F32),
        ],
        flops=1 << 31,
        name="outer",
    )(idx, *mine, theirs, alignment_right, wbd)
    parts = [partial[0]] + [swap(partial[k], "depth", k) for k in range(1, groups)]

    pair_strip, normed = call(
        functools.partial(norm_kernel, 1.0 / (seqs * depth_count)),
        (
            jax.ShapeDtypeStruct((R_DEV, tokens, CZ), BF),
            jax.ShapeDtypeStruct((R_DEV, tokens, CZ), BF),
        ),
        [VMEM] * (groups + 1),
        [pltpu.VMEM((R_DEV * tokens, CZ), F32)],
        flops=1 << 24,
        name="norm",
    )(*parts, outer_product_bias[None, :])

    near = [normed] + [swap(normed, "res", 2 * k) for k in range(1, chips)]
    far = swap(jnp.stack(near), "res", 1)
    queries, gate = call(
        query_kernel,
        (
            jax.ShapeDtypeStruct((R_DEV * tokens, CZ), BF),
            jax.ShapeDtypeStruct((R_DEV * tokens, CZ), F32),
        ),
        [VMEM] * 2,
        flops=1 << 27,
        name="query",
    )(normed, query_key_value_gate_weight)
    update = call(
        functools.partial(attend_kernel, chips),
        jax.ShapeDtypeStruct((R_DEV, tokens, CZ), BF),
        [SMEM] + [VMEM] * (chips + 6),
        [
            pltpu.VMEM((R_DEV, keys, CZ), BF),
            pltpu.VMEM((R_DEV * tokens, CZ), BF),
        ],
        flops=1 << 29,
        name="attend",
    )(idx, *near, far, queries, gate, query_key_value_gate_weight, output_weight, bias)
    return (pair_strip, update)


def solution(mesh):
    in_specs = (
        P("depth", "res"),
        P("depth", "res"),
        P(),
        P(),
        P(),
        P(),
        P(),
        P(None, "res", None),
        P(),
        P(),
    )
    out_specs = (P("depth", "res", None), P("depth", "res", None))
    return jax.shard_map(body, mesh=mesh, in_specs=in_specs, out_specs=out_specs, check_vma=False)
```

```python
import functools

import jax
import jax.numpy as jnp
from jax import lax
from jax.experimental import pallas as pl
from jax.experimental.pallas import tpu as pltpu
from jax.sharding import PartitionSpec as P


PROJ_CHANNELS = 32
CZ = 128
H = 4
DH = 32
R_DEV = 8
LANES = 128
PACK = LANES // PROJ_CHANNELS
WINDOW = R_DEV * PROJ_CHANNELS
SPAN = WINDOW + LANES


epsilon = 1e-05
VMEM = pl.BlockSpec(memory_space=pltpu.VMEM)
SMEM = pl.BlockSpec(memory_space=pltpu.SMEM)
BF = jnp.bfloat16
F32 = jnp.float32


def call(kernel, outs, specs, scratch=(), flops=0, limit=8):
    return pl.pallas_call(
        kernel,
        out_shape=outs,
        in_specs=specs,
        out_specs=[VMEM] * len(outs),
        scratch_shapes=list(scratch),
        compiler_params=pltpu.CompilerParams(vmem_limit_bytes=limit << 20),
        cost_estimate=pl.CostEstimate(
            flops=flops, bytes_accessed=1 << 20, transcendentals=0
        ),
    )


def prep_kernel(idx, off, w_ref, tri_ref, chain_ref, right_ref, wbd_ref, bias_ref, copy_ref):
    copy_ref[...] = right_ref[...]
    wbd_ref[...] = jnp.zeros_like(wbd_ref)
    for c in range(PROJ_CHANNELS):
        block = w_ref[c * PROJ_CHANNELS : (c + 1) * PROJ_CHANNELS, :]
        for j in range(PACK):
            row = c * LANES + j * PROJ_CHANNELS
            wbd_ref[row : row + PROJ_CHANNELS, j * CZ : (j + 1) * CZ] = block
    tokens, keys = tri_ref.shape[1:]
    first = idx[1] * tokens
    chain = jnp.broadcast_to(chain_ref[...], (tokens, keys))
    rows = lax.broadcasted_iota(jnp.int32, (tokens, keys), 0)
    cols = lax.broadcasted_iota(jnp.int32, (tokens, keys), 1)
    own = jnp.sum(jnp.where(cols == rows + first, chain, 0), axis=1, keepdims=True)
    differ = (chain != own).astype(F32)
    for h in range(H):
        bias_ref[h * tokens : (h + 1) * tokens, :] = (
            tri_ref[h].astype(F32) + off[h] * differ
        )


def select_kernel(idx, starts, own_ref, recv_ref, *refs):
    outs, chip_ref = refs[:-1], refs[-1]
    chips = len(outs)
    size, half = outs[0].shape
    width = own_ref.shape[1]
    res = idx[1]
    core = res % 2
    z = res // 2
    own_at = pl.multiple_of(core * width, LANES)
    recv_at = pl.multiple_of((1 - core) * width, LANES)
    seq_at = pl.multiple_of(core * half, half)
    chip_ref[:, pl.ds(own_at, width)] = own_ref[pl.ds(seq_at, half), :]
    chip_ref[:, pl.ds(recv_at, width)] = recv_ref[...]
    m = lax.broadcasted_iota(jnp.int32, (size, SPAN), 0)
    lane = lax.broadcasted_iota(jnp.int32, (size, SPAN), 1)
    delta = lane - (m % R_DEV) * PROJ_CHANNELS - m // R_DEV
    for k in range(chips):
        g = jnp.bitwise_xor(z, k)
        split = WINDOW // size
        first = g % split * (size // R_DEV)
        start = starts[g // split] * PROJ_CHANNELS - z * (2 * width)
        base = jnp.clip(start, 0, 2 * width - SPAN) // LANES * LANES
        base = pl.multiple_of(base, LANES)
        pick = (delta == start + first - base).astype(F32).astype(BF)
        outs[k][...] = lax.dot_general(
            pick,
            chip_ref[:, pl.ds(base, SPAN)],
            (((1,), (1,)), ((), ())),
            preferred_element_type=F32,
        ).astype(BF)


def outer_kernel(chips, idx, *refs):
    mine, theirs = refs[:chips], refs[chips : 2 * chips]
    b_ref, wbd_ref, *outs = refs[2 * chips : -3]
    at_ref, lhs_ref, acc_ref = refs[-3:]
    size, half = mine[0].shape
    groups = len(outs)
    z = idx[1] // 2
    core = idx[1] % 2
    mine_at = pl.multiple_of(core * half, LANES)
    theirs_at = pl.multiple_of((1 - core) * half, LANES)
    for k in range(chips):
        row = pl.multiple_of(jnp.bitwise_xor(z, k) * size, size)
        at_ref[pl.ds(row, size), pl.ds(mine_at, half)] = mine[k][...]
        at_ref[pl.ds(row, size), pl.ds(theirs_at, half)] = theirs[k][...]
    width = b_ref.shape[1]
    rows = groups * R_DEV
    for n in range(width // (2 * LANES)):
        part = jnp.dot(
            at_ref[...],
            b_ref[:, n * 2 * LANES : (n + 1) * 2 * LANES],
            preferred_element_type=F32,
        ).reshape(groups, PROJ_CHANNELS, R_DEV, 2 * LANES)
        for c in range(PROJ_CHANNELS):
            for q in range(2):
                slab = part[:, c, :, q * LANES : (q + 1) * LANES].reshape(rows, LANES)
                lhs_ref[
                    (2 * n + q) * rows : (2 * n + q + 1) * rows,
                    c * LANES : (c + 1) * LANES,
                ] = slab.astype(BF)
    acc = jnp.dot(lhs_ref[...], wbd_ref[...], preferred_element_type=F32)
    chunks = width // LANES
    acc_ref[...] = acc.reshape(chunks, groups, R_DEV, PACK * CZ)
    for k in range(groups):
        g = jnp.bitwise_xor(idx[0], k)
        block = acc_ref[:, g]
        block = jnp.stack(
            [block[:, :, j * CZ : (j + 1) * CZ] for j in range(PACK)], axis=1
        )
        outs[k][...] = block.reshape(chunks * PACK * R_DEV, CZ).astype(BF)


def norm_kernel(scale, *refs):
    parts = refs[:-4]
    bias_ref, pair_ref, normed_ref, sum_ref = refs[-4:]
    total = parts[0][...].astype(F32)
    for p in parts[1:]:
        total = total + p[...].astype(F32)
    sum_ref[...] = total * scale + bias_ref[...]
    tokens = pair_ref.shape[1]
    for u in range(R_DEV):
        pair = sum_ref[pl.ds(u, tokens, stride=R_DEV), :].astype(BF)
        pair_ref[u] = pair
        values = pair.astype(F32)
        centred = values - jnp.mean(values, axis=-1, keepdims=True)
        variance = jnp.mean(centred * centred, axis=-1, keepdims=True)
        normed_ref[u] = (centred * lax.rsqrt(variance + epsilon)).astype(BF)


def query_kernel(normed_ref, w_ref, q_ref, gate_ref):
    rows = R_DEV * normed_ref.shape[1]
    x = normed_ref[...].reshape(rows, CZ)
    q_ref[...] = jnp.dot(x, w_ref[:, :CZ], preferred_element_type=F32).astype(BF)
    g = jnp.dot(x, w_ref[:, 3 * CZ :], preferred_element_type=F32).astype(BF)
    gate_ref[...] = jax.nn.sigmoid(g.astype(F32))


def attend_kernel(chips, idx, *refs):
    mine, theirs = refs[:chips], refs[chips : 2 * chips]
    q_ref, gate_ref, w_ref, wo_ref, bias_ref, out_ref, all_ref, gated_ref = refs[2 * chips :]
    tokens = mine[0].shape[1]
    z = idx[1] // 2
    core = idx[1] % 2
    for k in range(chips):
        chip = jnp.bitwise_xor(z, k) * 2
        mine_at = pl.multiple_of((chip + core) * tokens, tokens)
        theirs_at = pl.multiple_of((chip + 1 - core) * tokens, tokens)
        all_ref[:, pl.ds(mine_at, tokens), :] = mine[k][...]
        all_ref[:, pl.ds(theirs_at, tokens), :] = theirs[k][...]
    scale = DH ** (-0.5)
    lane_head = lax.broadcasted_iota(jnp.int32, (tokens, CZ), 1) // DH
    for u in range(R_DEV):
        kv = jnp.dot(
            all_ref[u], w_ref[:, CZ : 3 * CZ], preferred_element_type=F32
        ).astype(BF)
        q = q_ref[u * tokens : (u + 1) * tokens, :]
        spread = jnp.concatenate(
            [jnp.where(lane_head == h, q, jnp.zeros_like(q)) for h in range(H)], axis=0
        )
        scores = lax.dot_general(
            spread, kv[:, :CZ], (((1,), (1,)), ((), ())), preferred_element_type=F32
        )
        scores = scores * scale + bias_ref[...]
        weights = jnp.exp(scores - jnp.max(scores, axis=-1, keepdims=True))
        denom = jnp.sum(weights, axis=-1, keepdims=True)
        value = jnp.dot(weights.astype(BF), kv[:, CZ:], preferred_element_type=F32)
        value = value / denom
        attended = jnp.zeros((tokens, CZ), F32)
        for h in range(H):
            attended = jnp.where(
                lane_head == h, value[h * tokens : (h + 1) * tokens, :], attended
            )
        gated_ref[u * tokens : (u + 1) * tokens, :] = (
            gate_ref[u * tokens : (u + 1) * tokens, :] * attended
        ).astype(BF)
    out = jnp.dot(gated_ref[...], wo_ref[...], preferred_element_type=F32)
    out_ref[...] = out.astype(BF).reshape(R_DEV, tokens, CZ)


def swap(x, axis, mask):
    n = lax.axis_size(axis)
    return lax.ppermute(x, axis, [(i, i ^ mask) for i in range(n)])


def body(
    alignment_left,
    alignment_right,
    window_starts,
    outer_product_weight,
    outer_product_bias,
    query_key_value_gate_weight,
    output_weight,
    triangle_pair_bias,
    residue_chain,
    interchain_offset,
):
    depth_count = lax.axis_size("depth")
    res_count = lax.axis_size("res")
    groups = window_starts.shape[0]
    chips = res_count // 2
    size = groups * WINDOW // chips
    assert groups == depth_count and WINDOW % size == 0
    seqs, width = alignment_left.shape
    half = seqs // 2
    tokens = width // PROJ_CHANNELS
    keys = residue_chain.shape[0]
    rows = groups * R_DEV
    res = lax.axis_index("res")
    idx = jnp.stack([lax.axis_index("depth"), res]).astype(jnp.int32)

    core = res % 2
    sent = lax.dynamic_slice_in_dim(alignment_left, (1 - core) * half, half, 0)
    recv = swap(sent, "res", 1)

    wbd, bias, right = call(
        prep_kernel,
        [
            pltpu.VMEM((PROJ_CHANNELS * LANES, PACK * CZ), BF),
            pltpu.VMEM((H * tokens, keys), F32),
            pltpu.VMEM(alignment_right.shape, BF),
        ],
        [SMEM, SMEM, VMEM, VMEM, VMEM, VMEM],
        flops=1 << 28,
    )(idx, interchain_offset, outer_product_weight, triangle_pair_bias, residue_chain[None, :], alignment_right)

    picked = call(
        select_kernel,
        [pltpu.VMEM((size, half), BF)] * chips,
        [SMEM, SMEM, VMEM, VMEM],
        [pltpu.VMEM((half, 2 * width), BF)],
        flops=1 << 28,
    )(idx, window_starts, alignment_left, recv)
    piece = picked[0]
    for k in range(1, chips):
        piece = piece + swap(picked[k], "res", 2 * k)
    mine = [piece] + [swap(piece, "res", 2 * k) for k in range(1, chips)]
    theirs = [swap(m, "res", 1) for m in mine]

    partial = call(
        functools.partial(outer_kernel, chips),
        [pltpu.VMEM((R_DEV * tokens, CZ), BF)] * groups,
        [SMEM] + [VMEM] * (2 * chips + 2),
        [
            pltpu.VMEM((groups * WINDOW, seqs), BF),
            pltpu.VMEM((rows * width // LANES, PROJ_CHANNELS * LANES), BF),
            pltpu.VMEM((width // LANES, groups, R_DEV, PACK * CZ), F32),
        ],
        flops=1 << 31,
        limit=32,
    )(idx, *mine, *theirs, right, wbd)
    parts = [partial[0]] + [swap(partial[k], "depth", k) for k in range(1, groups)]

    pair_strip, normed = call(
        functools.partial(norm_kernel, 1.0 / (seqs * depth_count)),
        [
            jax.ShapeDtypeStruct((R_DEV, tokens, CZ), BF),
            pltpu.VMEM((R_DEV, tokens, CZ), BF),
        ],
        [VMEM] * (groups + 1),
        [pltpu.VMEM((R_DEV * tokens, CZ), F32)],
        flops=1 << 24,
    )(*parts, outer_product_bias[None, :])

    near = [normed] + [swap(normed, "res", 2 * k) for k in range(1, chips)]
    far = [swap(n, "res", 1) for n in near]
    queries, gate = call(
        query_kernel,
        [
            pltpu.VMEM((R_DEV * tokens, CZ), BF),
            pltpu.VMEM((R_DEV * tokens, CZ), F32),
        ],
        [VMEM] * 2,
        flops=1 << 27,
    )(normed, query_key_value_gate_weight)
    (update,) = call(
        functools.partial(attend_kernel, chips),
        [jax.ShapeDtypeStruct((R_DEV, tokens, CZ), BF)],
        [SMEM] + [VMEM] * (2 * chips + 5),
        [
            pltpu.VMEM((R_DEV, keys, CZ), BF),
            pltpu.VMEM((R_DEV * tokens, CZ), BF),
        ],
        flops=1 << 29,
        limit=16,
    )(idx, *near, *far, queries, gate, query_key_value_gate_weight, output_weight, bias)
    return (pair_strip, update)


def solution(mesh):
    in_specs = (
        P("depth", "res"),
        P("depth", "res"),
        P(),
        P(),
        P(),
        P(),
        P(),
        P(None, "res", None),
        P(),
        P(),
    )
    out_specs = (P("depth", "res", None), P("depth", "res", None))
    return jax.shard_map(body, mesh=mesh, in_specs=in_specs, out_specs=out_specs, check_vma=False)
```

```python
import functools

import jax
import jax.numpy as jnp
from jax import lax
from jax.experimental import pallas as pl
from jax.experimental.pallas import tpu as pltpu
from jax.sharding import PartitionSpec as P


PROJ_CHANNELS = 32
CZ = 128
H = 4
DH = 32
R_DEV = 8
LANES = 128
PACK = LANES // PROJ_CHANNELS
WINDOW = R_DEV * PROJ_CHANNELS
SPAN = WINDOW + LANES


epsilon = 1e-05
VMEM = pl.BlockSpec(memory_space=pltpu.VMEM)
SMEM = pl.BlockSpec(memory_space=pltpu.SMEM)
ANY = pl.BlockSpec(memory_space=pltpu.HBM)
BF = jnp.bfloat16
F32 = jnp.float32


def call(kernel, outs, specs, scratch=(), flops=0, limit=8):
    return pl.pallas_call(
        kernel,
        out_shape=outs,
        in_specs=specs,
        out_specs=[
            SMEM if getattr(o, "memory_space", None) == pltpu.SMEM else VMEM for o in outs
        ],
        scratch_shapes=list(scratch),
        compiler_params=pltpu.CompilerParams(vmem_limit_bytes=limit << 20),
        cost_estimate=pl.CostEstimate(
            flops=flops, bytes_accessed=1 << 20, transcendentals=0
        ),
    )


def front_kernel(left_ref, starts_ref, sent_ref, kept_ref, table_ref, sem):
    half = sent_ref.shape[0]
    core = lax.axis_index("res") % 2
    sent_at = pl.multiple_of((1 - core) * half, half)
    kept_at = pl.multiple_of(core * half, half)
    copies = [
        pltpu.make_async_copy(left_ref.at[pl.ds(sent_at, half)], sent_ref, sem.at[0]),
        pltpu.make_async_copy(left_ref.at[pl.ds(kept_at, half)], kept_ref, sem.at[1]),
        pltpu.make_async_copy(starts_ref, table_ref, sem.at[2]),
    ]
    for copy in copies:
        copy.start()
    for copy in copies:
        copy.wait()


def prep_kernel(*refs):
    sources, outs, scratch = refs[:8], refs[8:14], refs[14:]
    wbd_ref, bias_ref = outs[:2]
    w_ref, tri_ref, chain_ref, off_ref, sem = scratch
    targets = [w_ref, tri_ref, chain_ref, off_ref, *outs[2:]]
    copies = [
        pltpu.make_async_copy(a, b, sem.at[n])
        for n, (a, b) in enumerate(zip(sources, targets))
    ]
    for copy in copies:
        copy.start()
    wbd_ref[...] = jnp.zeros_like(wbd_ref)
    for copy in copies:
        copy.wait()
    for c in range(PROJ_CHANNELS):
        block = w_ref[c * PROJ_CHANNELS : (c + 1) * PROJ_CHANNELS, :]
        for j in range(PACK):
            row = c * LANES + j * PROJ_CHANNELS
            wbd_ref[row : row + PROJ_CHANNELS, j * CZ : (j + 1) * CZ] = block
    tokens, keys = tri_ref.shape[1:]
    first = lax.axis_index("res") * tokens
    chain = jnp.broadcast_to(chain_ref[...], (tokens, keys))
    rows = lax.broadcasted_iota(jnp.int32, (tokens, keys), 0)
    cols = lax.broadcasted_iota(jnp.int32, (tokens, keys), 1)
    own = jnp.sum(jnp.where(cols == rows + first, chain, 0), axis=1, keepdims=True)
    differ = (chain != own).astype(F32)
    for h in range(H):
        bias_ref[h * tokens : (h + 1) * tokens, :] = (
            tri_ref[h].astype(F32) + off_ref[h] * differ
        )


def select_kernel(starts, own_ref, recv_ref, *refs):
    outs, chip_ref = refs[:-1], refs[-1]
    chips = len(outs)
    size, _ = outs[0].shape
    width = own_ref.shape[1]
    res = lax.axis_index("res")
    core = res % 2
    z = res // 2
    own_at = pl.multiple_of(core * width, LANES)
    recv_at = pl.multiple_of((1 - core) * width, LANES)
    chip_ref[:, pl.ds(own_at, width)] = own_ref[...]
    chip_ref[:, pl.ds(recv_at, width)] = recv_ref[...]
    m = lax.broadcasted_iota(jnp.int32, (size, SPAN), 0)
    lane = lax.broadcasted_iota(jnp.int32, (size, SPAN), 1)
    delta = lane - (m % R_DEV) * PROJ_CHANNELS - m // R_DEV
    for k in range(chips):
        g = jnp.bitwise_xor(z, k)
        split = WINDOW // size
        first = g % split * (size // R_DEV)
        start = starts[g // split] * PROJ_CHANNELS - z * (2 * width)
        base = jnp.clip(start, 0, 2 * width - SPAN) // LANES * LANES
        base = pl.multiple_of(base, LANES)
        pick = (delta == start + first - base).astype(F32).astype(BF)
        outs[k][...] = lax.dot_general(
            pick,
            chip_ref[:, pl.ds(base, SPAN)],
            (((1,), (1,)), ((), ())),
            preferred_element_type=F32,
        ).astype(BF)


def outer_kernel(chips, *refs):
    mine, theirs = refs[:chips], refs[chips : 2 * chips]
    b_ref, wbd_ref, *outs = refs[2 * chips : -3]
    at_ref, lhs_ref, acc_ref = refs[-3:]
    size, half = mine[0].shape
    groups = len(outs)
    z = lax.axis_index("res") // 2
    core = lax.axis_index("res") % 2
    mine_at = pl.multiple_of(core * half, LANES)
    theirs_at = pl.multiple_of((1 - core) * half, LANES)
    for k in range(chips):
        row = pl.multiple_of(jnp.bitwise_xor(z, k) * size, size)
        at_ref[pl.ds(row, size), pl.ds(mine_at, half)] = mine[k][...]
        at_ref[pl.ds(row, size), pl.ds(theirs_at, half)] = theirs[k][...]
    width = b_ref.shape[1]
    rows = groups * R_DEV
    for n in range(width // (2 * LANES)):
        part = jnp.dot(
            at_ref[...],
            b_ref[:, n * 2 * LANES : (n + 1) * 2 * LANES],
            preferred_element_type=F32,
        ).reshape(groups, PROJ_CHANNELS, R_DEV, 2 * LANES)
        for c in range(PROJ_CHANNELS):
            for q in range(2):
                slab = part[:, c, :, q * LANES : (q + 1) * LANES].reshape(rows, LANES)
                lhs_ref[
                    (2 * n + q) * rows : (2 * n + q + 1) * rows,
                    c * LANES : (c + 1) * LANES,
                ] = slab.astype(BF)
    acc = jnp.dot(lhs_ref[...], wbd_ref[...], preferred_element_type=F32)
    chunks = width // LANES
    acc_ref[...] = acc.reshape(chunks, groups, R_DEV, PACK * CZ)
    for k in range(groups):
        g = jnp.bitwise_xor(lax.axis_index("depth"), k)
        block = acc_ref[:, g]
        block = jnp.stack(
            [block[:, :, j * CZ : (j + 1) * CZ] for j in range(PACK)], axis=1
        )
        outs[k][...] = block.reshape(chunks * PACK * R_DEV, CZ).astype(BF)


def norm_kernel(scale, *refs):
    parts = refs[:-4]
    bias_ref, pair_ref, normed_ref, sum_ref = refs[-4:]
    total = parts[0][...].astype(F32)
    for p in parts[1:]:
        total = total + p[...].astype(F32)
    sum_ref[...] = total * scale + bias_ref[...]
    tokens = pair_ref.shape[1]
    for u in range(R_DEV):
        pair = sum_ref[pl.ds(u, tokens, stride=R_DEV), :].astype(BF)
        pair_ref[u] = pair
        values = pair.astype(F32)
        centred = values - jnp.mean(values, axis=-1, keepdims=True)
        variance = jnp.mean(centred * centred, axis=-1, keepdims=True)
        normed_ref[u] = (centred * lax.rsqrt(variance + epsilon)).astype(BF)


def query_kernel(normed_ref, w_ref, q_ref, gate_ref):
    rows = R_DEV * normed_ref.shape[1]
    x = normed_ref[...].reshape(rows, CZ)
    q_ref[...] = jnp.dot(x, w_ref[:, :CZ], preferred_element_type=F32).astype(BF)
    g = jnp.dot(x, w_ref[:, 3 * CZ :], preferred_element_type=F32).astype(BF)
    gate_ref[...] = jax.nn.sigmoid(g.astype(F32))


def attend_kernel(chips, *refs):
    mine, theirs = refs[:chips], refs[chips : 2 * chips]
    q_ref, gate_ref, w_ref, wo_ref, bias_ref, out_ref, all_ref, gated_ref = refs[2 * chips :]
    tokens = mine[0].shape[1]
    z = lax.axis_index("res") // 2
    core = lax.axis_index("res") % 2
    for k in range(chips):
        chip = jnp.bitwise_xor(z, k) * 2
        mine_at = pl.multiple_of((chip + core) * tokens, tokens)
        theirs_at = pl.multiple_of((chip + 1 - core) * tokens, tokens)
        all_ref[:, pl.ds(mine_at, tokens), :] = mine[k][...]
        all_ref[:, pl.ds(theirs_at, tokens), :] = theirs[k][...]
    scale = DH ** (-0.5)
    lane_head = lax.broadcasted_iota(jnp.int32, (tokens, CZ), 1) // DH
    for u in range(R_DEV):
        kv = jnp.dot(
            all_ref[u], w_ref[:, CZ : 3 * CZ], preferred_element_type=F32
        ).astype(BF)
        q = q_ref[u * tokens : (u + 1) * tokens, :]
        spread = jnp.concatenate(
            [jnp.where(lane_head == h, q, jnp.zeros_like(q)) for h in range(H)], axis=0
        )
        scores = lax.dot_general(
            spread, kv[:, :CZ], (((1,), (1,)), ((), ())), preferred_element_type=F32
        )
        scores = scores * scale + bias_ref[...]
        weights = jnp.exp(scores - jnp.max(scores, axis=-1, keepdims=True))
        denom = jnp.sum(weights, axis=-1, keepdims=True)
        value = jnp.dot(weights.astype(BF), kv[:, CZ:], preferred_element_type=F32)
        value = value / denom
        attended = jnp.zeros((tokens, CZ), F32)
        for h in range(H):
            attended = jnp.where(
                lane_head == h, value[h * tokens : (h + 1) * tokens, :], attended
            )
        gated_ref[u * tokens : (u + 1) * tokens, :] = (
            gate_ref[u * tokens : (u + 1) * tokens, :] * attended
        ).astype(BF)
    out = jnp.dot(gated_ref[...], wo_ref[...], preferred_element_type=F32)
    out_ref[...] = out.astype(BF).reshape(R_DEV, tokens, CZ)


def in_hbm(*arrays):
    return [pltpu.with_memory_space_constraint(a, pltpu.HBM) for a in arrays]


def swap(x, axis, mask):
    n = lax.axis_size(axis)
    return lax.ppermute(x, axis, [(i, i ^ mask) for i in range(n)])


def body(
    alignment_left,
    alignment_right,
    window_starts,
    outer_product_weight,
    outer_product_bias,
    query_key_value_gate_weight,
    output_weight,
    triangle_pair_bias,
    residue_chain,
    interchain_offset,
):
    depth_count = lax.axis_size("depth")
    res_count = lax.axis_size("res")
    groups = window_starts.shape[0]
    chips = res_count // 2
    size = groups * WINDOW // chips
    assert groups == depth_count and WINDOW % size == 0
    seqs, width = alignment_left.shape
    half = seqs // 2
    tokens = width // PROJ_CHANNELS
    keys = residue_chain.shape[0]
    rows = groups * R_DEV

    sent, kept, table = call(
        front_kernel,
        [
            pltpu.VMEM((half, width), BF),
            pltpu.VMEM((half, width), BF),
            pltpu.SMEM(window_starts.shape, jnp.int32),
        ],
        [ANY, ANY],
        [pltpu.SemaphoreType.DMA((3,))],
    )(*in_hbm(alignment_left, window_starts))
    recv = swap(sent, "res", 1)

    wbd, bias, right, qkvg, wo, shift = call(
        prep_kernel,
        [
            pltpu.VMEM((PROJ_CHANNELS * LANES, PACK * CZ), BF),
            pltpu.VMEM((H * tokens, keys), F32),
            pltpu.VMEM(alignment_right.shape, BF),
            pltpu.VMEM(query_key_value_gate_weight.shape, BF),
            pltpu.VMEM(output_weight.shape, BF),
            pltpu.VMEM((1, CZ), F32),
        ],
        [ANY] * 8,
        [
            pltpu.VMEM(outer_product_weight.shape, BF),
            pltpu.VMEM(triangle_pair_bias.shape, BF),
            pltpu.VMEM((1, keys), jnp.int32),
            pltpu.SMEM((H,), F32),
            pltpu.SemaphoreType.DMA((8,)),
        ],
        flops=1 << 28,
    )(
        *in_hbm(
            outer_product_weight,
            triangle_pair_bias,
            residue_chain[None, :],
            interchain_offset,
            alignment_right,
            query_key_value_gate_weight,
            output_weight,
            outer_product_bias[None, :],
        )
    )

    picked = call(
        select_kernel,
        [pltpu.VMEM((size, half), BF)] * chips,
        [SMEM, VMEM, VMEM],
        [pltpu.VMEM((half, 2 * width), BF)],
        flops=1 << 28,
    )(table, kept, recv)
    piece = picked[0]
    for k in range(1, chips):
        piece = piece + swap(picked[k], "res", 2 * k)
    mine = [piece] + [swap(piece, "res", 2 * k) for k in range(1, chips)]
    theirs = [swap(m, "res", 1) for m in mine]

    partial = call(
        functools.partial(outer_kernel, chips),
        [pltpu.VMEM((R_DEV * tokens, CZ), BF)] * groups,
        [VMEM] * (2 * chips + 2),
        [
            pltpu.VMEM((groups * WINDOW, seqs), BF),
            pltpu.VMEM((rows * width // LANES, PROJ_CHANNELS * LANES), BF),
            pltpu.VMEM((width // LANES, groups, R_DEV, PACK * CZ), F32),
        ],
        flops=1 << 31,
        limit=32,
    )(*mine, *theirs, right, wbd)
    parts = [partial[0]] + [swap(partial[k], "depth", k) for k in range(1, groups)]

    pair_strip, normed = call(
        functools.partial(norm_kernel, 1.0 / (seqs * depth_count)),
        [
            jax.ShapeDtypeStruct((R_DEV, tokens, CZ), BF),
            pltpu.VMEM((R_DEV, tokens, CZ), BF),
        ],
        [VMEM] * (groups + 1),
        [pltpu.VMEM((R_DEV * tokens, CZ), F32)],
        flops=1 << 24,
    )(*parts, shift)

    near = [normed] + [swap(normed, "res", 2 * k) for k in range(1, chips)]
    far = [swap(n, "res", 1) for n in near]
    queries, gate = call(
        query_kernel,
        [
            pltpu.VMEM((R_DEV * tokens, CZ), BF),
            pltpu.VMEM((R_DEV * tokens, CZ), F32),
        ],
        [VMEM] * 2,
        flops=1 << 27,
    )(normed, qkvg)
    (update,) = call(
        functools.partial(attend_kernel, chips),
        [jax.ShapeDtypeStruct((R_DEV, tokens, CZ), BF)],
        [VMEM] * (2 * chips + 5),
        [
            pltpu.VMEM((R_DEV, keys, CZ), BF),
            pltpu.VMEM((R_DEV * tokens, CZ), BF),
        ],
        flops=1 << 29,
        limit=16,
    )(*near, *far, queries, gate, qkvg, wo, bias)
    return (pair_strip, update)


def solution(mesh):
    in_specs = (
        P("depth", "res"),
        P("depth", "res"),
        P(),
        P(),
        P(),
        P(),
        P(),
        P(None, "res", None),
        P(),
        P(),
    )
    out_specs = (P("depth", "res", None), P("depth", "res", None))
    return jax.shard_map(body, mesh=mesh, in_specs=in_specs, out_specs=out_specs, check_vma=False)
```

```python
import functools
import itertools

import jax
import jax.numpy as jnp
from jax import lax
from jax.experimental import pallas as pl
from jax.experimental.pallas import tpu as pltpu
from jax.sharding import PartitionSpec as P


PROJ_CHANNELS = 32
CZ = 128
H = 4
DH = 32
R_DEV = 8
LANES = 128
PACK = LANES // PROJ_CHANNELS
WINDOW = R_DEV * PROJ_CHANNELS
SPAN = WINDOW + LANES


epsilon = 1e-05
VMEM = pl.BlockSpec(memory_space=pltpu.VMEM)
SMEM = pl.BlockSpec(memory_space=pltpu.SMEM)
ANY = pl.BlockSpec(memory_space=pltpu.HBM)
BF = jnp.bfloat16
F32 = jnp.float32


def call(kernel, outs, specs, scratch=(), flops=0, limit=8):
    return pl.pallas_call(
        kernel,
        out_shape=outs,
        in_specs=specs,
        out_specs=[
            SMEM if getattr(o, "memory_space", None) == pltpu.SMEM else VMEM for o in outs
        ],
        scratch_shapes=list(scratch),
        compiler_params=pltpu.CompilerParams(vmem_limit_bytes=limit << 20),
        cost_estimate=pl.CostEstimate(
            flops=flops, bytes_accessed=1 << 20, transcendentals=0
        ),
    )


def front_kernel(adaptive, chip_tokens, left_ref, starts_ref, sent_ref, kept_ref, table_ref, need_ref, raw_ref, sem):
    half = sent_ref.shape[0]
    core = lax.axis_index("res") % 2
    sent_at = pl.multiple_of((1 - core) * half, half)
    kept_at = pl.multiple_of(core * half, half)
    copies = [
        pltpu.make_async_copy(starts_ref, raw_ref, sem.at[0]),
        pltpu.make_async_copy(left_ref.at[pl.ds(sent_at, half)], sent_ref, sem.at[1]),
        pltpu.make_async_copy(left_ref.at[pl.ds(kept_at, half)], kept_ref, sem.at[2]),
    ]
    for copy in copies:
        copy.start()
    copies[0].wait()
    groups = starts_ref.shape[0]
    need_ref[0] = 0
    for g in range(groups):
        table_ref[g] = g
    if adaptive:
        starts = [raw_ref[g] for g in range(groups)]
        reach = []
        for start in starts:
            low = start // chip_tokens
            high = (start + (R_DEV - 1)) // chip_tokens
            reach.append(
                [
                    jnp.left_shift(1, jnp.bitwise_xor(low, h))
                    | jnp.left_shift(1, jnp.bitwise_xor(high, h))
                    for h in range(groups)
                ]
            )
        best = cost = homes = None
        for order in itertools.permutations(range(groups)):
            mask = functools.reduce(
                jnp.bitwise_or, [reach[w][h] for h, w in enumerate(order)]
            )
            price = sum((jnp.right_shift(mask, k) & 1) * (4 if k == 1 else 5) for k in range(1, groups))
            packed = jnp.int32(sum(w << (4 * h) for h, w in enumerate(order)))
            if best is None:
                best, cost, homes = mask, price, packed
            else:
                better = price < cost
                best = jnp.where(better, mask, best)
                homes = jnp.where(better, packed, homes)
                cost = jnp.where(better, price, cost)
        need_ref[0] = jnp.right_shift(best, 1)
        for h in range(groups):
            table_ref[h] = jnp.right_shift(homes, 4 * h) & 15
    for g in range(groups):
        table_ref[groups + g] = raw_ref[table_ref[g]]
    for copy in copies[1:]:
        copy.wait()


def prep_kernel(*refs):
    sources, outs, scratch = refs[:8], refs[8:14], refs[14:]
    wbd_ref, bias_ref = outs[:2]
    w_ref, tri_ref, chain_ref, off_ref, sem = scratch
    targets = [w_ref, tri_ref, chain_ref, off_ref, *outs[2:]]
    copies = [
        pltpu.make_async_copy(a, b, sem.at[n])
        for n, (a, b) in enumerate(zip(sources, targets))
    ]
    for copy in copies:
        copy.start()
    wbd_ref[...] = jnp.zeros_like(wbd_ref)
    for copy in copies:
        copy.wait()
    for c in range(PROJ_CHANNELS):
        block = w_ref[c * PROJ_CHANNELS : (c + 1) * PROJ_CHANNELS, :]
        for j in range(PACK):
            row = c * LANES + j * PROJ_CHANNELS
            wbd_ref[row : row + PROJ_CHANNELS, j * CZ : (j + 1) * CZ] = block
    tokens, keys = tri_ref.shape[1:]
    first = lax.axis_index("res") * tokens
    chain = jnp.broadcast_to(chain_ref[...], (tokens, keys))
    rows = lax.broadcasted_iota(jnp.int32, (tokens, keys), 0)
    cols = lax.broadcasted_iota(jnp.int32, (tokens, keys), 1)
    own = jnp.sum(jnp.where(cols == rows + first, chain, 0), axis=1, keepdims=True)
    differ = (chain != own).astype(F32)
    for h in range(H):
        bias_ref[h * tokens : (h + 1) * tokens, :] = (
            tri_ref[h].astype(F32) + off_ref[h] * differ
        )


def select_kernel(table, own_ref, recv_ref, *refs):
    outs, chip_ref = refs[:-1], refs[-1]
    chips = len(outs)
    size, _ = outs[0].shape
    width = own_ref.shape[1]
    res = lax.axis_index("res")
    core = res % 2
    z = res // 2
    own_at = pl.multiple_of(core * width, LANES)
    recv_at = pl.multiple_of((1 - core) * width, LANES)
    chip_ref[:, pl.ds(own_at, width)] = own_ref[...]
    chip_ref[:, pl.ds(recv_at, width)] = recv_ref[...]
    m = lax.broadcasted_iota(jnp.int32, (size, SPAN), 0)
    lane = lax.broadcasted_iota(jnp.int32, (size, SPAN), 1)
    delta = lane - (m % R_DEV) * PROJ_CHANNELS - m // R_DEV
    split = WINDOW // size
    groups = chips // split
    for k in range(chips):
        at = jnp.bitwise_xor(z, k)
        first = at % split * (size // R_DEV)
        start = table[groups + at // split] * PROJ_CHANNELS - z * (2 * width)
        base = jnp.clip(start, 0, 2 * width - SPAN) // LANES * LANES
        base = pl.multiple_of(base, LANES)
        pick = (delta == start + first - base).astype(F32).astype(BF)
        outs[k][...] = lax.dot_general(
            pick,
            chip_ref[:, pl.ds(base, SPAN)],
            (((1,), (1,)), ((), ())),
            preferred_element_type=F32,
        ).astype(BF)


def outer_kernel(chips, table, *refs):
    mine, theirs = refs[:chips], refs[chips : 2 * chips]
    b_ref, wbd_ref, *outs = refs[2 * chips : -3]
    at_ref, lhs_ref, acc_ref = refs[-3:]
    size, half = mine[0].shape
    groups = len(outs)
    z = lax.axis_index("res") // 2
    core = lax.axis_index("res") % 2
    mine_at = pl.multiple_of(core * half, LANES)
    theirs_at = pl.multiple_of((1 - core) * half, LANES)
    for k in range(chips):
        at = jnp.bitwise_xor(z, k)
        split = WINDOW // size
        row = pl.multiple_of(table[at // split] * WINDOW + at % split * size, size)
        at_ref[pl.ds(row, size), pl.ds(mine_at, half)] = mine[k][...]
        at_ref[pl.ds(row, size), pl.ds(theirs_at, half)] = theirs[k][...]
    width = b_ref.shape[1]
    rows = groups * R_DEV
    for n in range(width // (2 * LANES)):
        part = jnp.dot(
            at_ref[...],
            b_ref[:, n * 2 * LANES : (n + 1) * 2 * LANES],
            preferred_element_type=F32,
        ).reshape(groups, PROJ_CHANNELS, R_DEV, 2 * LANES)
        for c in range(PROJ_CHANNELS):
            for q in range(2):
                slab = part[:, c, :, q * LANES : (q + 1) * LANES].reshape(rows, LANES)
                lhs_ref[
                    (2 * n + q) * rows : (2 * n + q + 1) * rows,
                    c * LANES : (c + 1) * LANES,
                ] = slab.astype(BF)
    acc = jnp.dot(lhs_ref[...], wbd_ref[...], preferred_element_type=F32)
    chunks = width // LANES
    acc_ref[...] = acc.reshape(chunks, groups, R_DEV, PACK * CZ)
    for k in range(groups):
        g = jnp.bitwise_xor(lax.axis_index("depth"), k)
        block = acc_ref[:, g]
        block = jnp.stack(
            [block[:, :, j * CZ : (j + 1) * CZ] for j in range(PACK)], axis=1
        )
        outs[k][...] = block.reshape(chunks * PACK * R_DEV, CZ).astype(BF)


def norm_kernel(scale, *refs):
    parts = refs[:-4]
    bias_ref, pair_ref, normed_ref, sum_ref = refs[-4:]
    total = parts[0][...].astype(F32)
    for p in parts[1:]:
        total = total + p[...].astype(F32)
    sum_ref[...] = total * scale + bias_ref[...]
    tokens = pair_ref.shape[1]
    for u in range(R_DEV):
        pair = sum_ref[pl.ds(u, tokens, stride=R_DEV), :].astype(BF)
        pair_ref[u] = pair
        values = pair.astype(F32)
        centred = values - jnp.mean(values, axis=-1, keepdims=True)
        variance = jnp.mean(centred * centred, axis=-1, keepdims=True)
        normed_ref[u] = (centred * lax.rsqrt(variance + epsilon)).astype(BF)


def query_kernel(normed_ref, w_ref, q_ref, gate_ref):
    rows = R_DEV * normed_ref.shape[1]
    x = normed_ref[...].reshape(rows, CZ)
    q_ref[...] = jnp.dot(x, w_ref[:, :CZ], preferred_element_type=F32).astype(BF)
    g = jnp.dot(x, w_ref[:, 3 * CZ :], preferred_element_type=F32).astype(BF)
    gate_ref[...] = jax.nn.sigmoid(g.astype(F32))


def attend_kernel(chips, *refs):
    mine, theirs = refs[:chips], refs[chips : 2 * chips]
    q_ref, gate_ref, w_ref, wo_ref, bias_ref, out_ref, all_ref, gated_ref = refs[2 * chips :]
    tokens = mine[0].shape[1]
    z = lax.axis_index("res") // 2
    core = lax.axis_index("res") % 2
    for k in range(chips):
        chip = jnp.bitwise_xor(z, k) * 2
        mine_at = pl.multiple_of((chip + core) * tokens, tokens)
        theirs_at = pl.multiple_of((chip + 1 - core) * tokens, tokens)
        all_ref[:, pl.ds(mine_at, tokens), :] = mine[k][...]
        all_ref[:, pl.ds(theirs_at, tokens), :] = theirs[k][...]
    scale = DH ** (-0.5)
    lane_head = lax.broadcasted_iota(jnp.int32, (tokens, CZ), 1) // DH
    for u in range(R_DEV):
        kv = jnp.dot(
            all_ref[u], w_ref[:, CZ : 3 * CZ], preferred_element_type=F32
        ).astype(BF)
        q = q_ref[u * tokens : (u + 1) * tokens, :]
        spread = jnp.concatenate(
            [jnp.where(lane_head == h, q, jnp.zeros_like(q)) for h in range(H)], axis=0
        )
        scores = lax.dot_general(
            spread, kv[:, :CZ], (((1,), (1,)), ((), ())), preferred_element_type=F32
        )
        scores = scores * scale + bias_ref[...]
        weights = jnp.exp(scores - jnp.max(scores, axis=-1, keepdims=True))
        denom = jnp.sum(weights, axis=-1, keepdims=True)
        value = jnp.dot(weights.astype(BF), kv[:, CZ:], preferred_element_type=F32)
        value = value / denom
        attended = jnp.zeros((tokens, CZ), F32)
        for h in range(H):
            attended = jnp.where(
                lane_head == h, value[h * tokens : (h + 1) * tokens, :], attended
            )
        gated_ref[u * tokens : (u + 1) * tokens, :] = (
            gate_ref[u * tokens : (u + 1) * tokens, :] * attended
        ).astype(BF)
    out = jnp.dot(gated_ref[...], wo_ref[...], preferred_element_type=F32)
    out_ref[...] = out.astype(BF).reshape(R_DEV, tokens, CZ)


def in_hbm(*arrays):
    return [pltpu.with_memory_space_constraint(a, pltpu.HBM) for a in arrays]


def swap(x, axis, mask):
    n = lax.axis_size(axis)
    return lax.ppermute(x, axis, [(i, i ^ mask) for i in range(n)])


def body(
    alignment_left,
    alignment_right,
    window_starts,
    outer_product_weight,
    outer_product_bias,
    query_key_value_gate_weight,
    output_weight,
    triangle_pair_bias,
    residue_chain,
    interchain_offset,
):
    depth_count = lax.axis_size("depth")
    res_count = lax.axis_size("res")
    groups = window_starts.shape[0]
    chips = res_count // 2
    size = groups * WINDOW // chips
    assert groups == depth_count and WINDOW % size == 0
    seqs, width = alignment_left.shape
    half = seqs // 2
    tokens = width // PROJ_CHANNELS
    keys = residue_chain.shape[0]
    rows = groups * R_DEV

    adaptive = chips == groups == 4
    sent, kept, table, need = call(
        functools.partial(front_kernel, adaptive, 2 * tokens),
        [
            pltpu.VMEM((half, width), BF),
            pltpu.VMEM((half, width), BF),
            pltpu.SMEM((2 * groups,), jnp.int32),
            pltpu.SMEM((1,), jnp.int32),
        ],
        [ANY, ANY],
        [pltpu.SMEM(window_starts.shape, jnp.int32), pltpu.SemaphoreType.DMA((3,))],
    )(*in_hbm(alignment_left, window_starts))
    recv = swap(sent, "res", 1)

    wbd, bias, right, qkvg, wo, shift = call(
        prep_kernel,
        [
            pltpu.VMEM((PROJ_CHANNELS * LANES, PACK * CZ), BF),
            pltpu.VMEM((H * tokens, keys), F32),
            pltpu.VMEM(alignment_right.shape, BF),
            pltpu.VMEM(query_key_value_gate_weight.shape, BF),
            pltpu.VMEM(output_weight.shape, BF),
            pltpu.VMEM((1, CZ), F32),
        ],
        [ANY] * 8,
        [
            pltpu.VMEM(outer_product_weight.shape, BF),
            pltpu.VMEM(triangle_pair_bias.shape, BF),
            pltpu.VMEM((1, keys), jnp.int32),
            pltpu.SMEM((H,), F32),
            pltpu.SemaphoreType.DMA((8,)),
        ],
        flops=1 << 28,
    )(
        *in_hbm(
            outer_product_weight,
            triangle_pair_bias,
            residue_chain[None, :],
            interchain_offset,
            alignment_right,
            query_key_value_gate_weight,
            output_weight,
            outer_product_bias[None, :],
        )
    )

    picked = call(
        select_kernel,
        [pltpu.VMEM((size, half), BF)] * chips,
        [SMEM, VMEM, VMEM],
        [pltpu.VMEM((half, 2 * width), BF)],
        flops=1 << 28,
    )(table, kept, recv)

    def collect(wanted, *picked):
        return functools.reduce(
            jnp.add,
            [picked[0]] + [swap(picked[k], "res", 2 * k) for k in wanted],
        )

    every = range(1, chips)
    if adaptive:
        subsets = [
            [k for k in every if bits >> (k - 1) & 1] for bits in range(1 << len(every))
        ]
        piece = lax.switch(
            need[0], [functools.partial(collect, wanted) for wanted in subsets], *picked
        )
    else:
        piece = collect(every, *picked)
    mine = [piece] + [swap(piece, "res", 2 * k) for k in range(1, chips)]
    theirs = [swap(m, "res", 1) for m in mine]

    partial = call(
        functools.partial(outer_kernel, chips),
        [pltpu.VMEM((R_DEV * tokens, CZ), BF)] * groups,
        [SMEM] + [VMEM] * (2 * chips + 2),
        [
            pltpu.VMEM((groups * WINDOW, seqs), BF),
            pltpu.VMEM((rows * width // LANES, PROJ_CHANNELS * LANES), BF),
            pltpu.VMEM((width // LANES, groups, R_DEV, PACK * CZ), F32),
        ],
        flops=1 << 31,
        limit=32,
    )(table, *mine, *theirs, right, wbd)
    parts = [partial[0]] + [swap(partial[k], "depth", k) for k in range(1, groups)]

    pair_strip, normed = call(
        functools.partial(norm_kernel, 1.0 / (seqs * depth_count)),
        [
            jax.ShapeDtypeStruct((R_DEV, tokens, CZ), BF),
            pltpu.VMEM((R_DEV, tokens, CZ), BF),
        ],
        [VMEM] * (groups + 1),
        [pltpu.VMEM((R_DEV * tokens, CZ), F32)],
        flops=1 << 24,
    )(*parts, shift)

    near = [normed] + [swap(normed, "res", 2 * k) for k in range(1, chips)]
    far = [swap(n, "res", 1) for n in near]
    queries, gate = call(
        query_kernel,
        [
            pltpu.VMEM((R_DEV * tokens, CZ), BF),
            pltpu.VMEM((R_DEV * tokens, CZ), F32),
        ],
        [VMEM] * 2,
        flops=1 << 27,
    )(normed, qkvg)
    (update,) = call(
        functools.partial(attend_kernel, chips),
        [jax.ShapeDtypeStruct((R_DEV, tokens, CZ), BF)],
        [VMEM] * (2 * chips + 5),
        [
            pltpu.VMEM((R_DEV, keys, CZ), BF),
            pltpu.VMEM((R_DEV * tokens, CZ), BF),
        ],
        flops=1 << 29,
        limit=16,
    )(*near, *far, queries, gate, qkvg, wo, bias)
    return (pair_strip, update)


def solution(mesh):
    in_specs = (
        P("depth", "res"),
        P("depth", "res"),
        P(),
        P(),
        P(),
        P(),
        P(),
        P(None, "res", None),
        P(),
        P(),
    )
    out_specs = (P("depth", "res", None), P("depth", "res", None))
    return jax.shard_map(body, mesh=mesh, in_specs=in_specs, out_specs=out_specs, check_vma=False)
```

```python
import functools
import itertools

import jax
import jax.numpy as jnp
from jax import lax
from jax.experimental import pallas as pl
from jax.experimental.pallas import tpu as pltpu
from jax.sharding import PartitionSpec as P


PROJ_CHANNELS = 32
CZ = 128
H = 4
DH = 32
R_DEV = 8
LANES = 128
PACK = LANES // PROJ_CHANNELS
WINDOW = R_DEV * PROJ_CHANNELS
SPAN = WINDOW + LANES


epsilon = 1e-05
VMEM = pl.BlockSpec(memory_space=pltpu.VMEM)
SMEM = pl.BlockSpec(memory_space=pltpu.SMEM)
ANY = pl.BlockSpec(memory_space=pltpu.HBM)
BF = jnp.bfloat16
F32 = jnp.float32


def call(kernel, outs, specs, scratch=(), flops=0, limit=8):
    return pl.pallas_call(
        kernel,
        out_shape=outs,
        in_specs=specs,
        out_specs=[
            SMEM if getattr(o, "memory_space", None) == pltpu.SMEM else VMEM for o in outs
        ],
        scratch_shapes=list(scratch),
        compiler_params=pltpu.CompilerParams(vmem_limit_bytes=limit << 20),
        cost_estimate=pl.CostEstimate(
            flops=flops, bytes_accessed=1 << 20, transcendentals=0
        ),
    )


def front_kernel(adaptive, chip_tokens, left_ref, starts_ref, sent_ref, kept_ref, table_ref, need_ref, raw_ref, sem):
    half = sent_ref.shape[0]
    core = lax.axis_index("res") % 2
    sent_at = pl.multiple_of((1 - core) * half, half)
    kept_at = pl.multiple_of(core * half, half)
    copies = [
        pltpu.make_async_copy(starts_ref, raw_ref, sem.at[0]),
        pltpu.make_async_copy(left_ref.at[pl.ds(sent_at, half)], sent_ref, sem.at[1]),
        pltpu.make_async_copy(left_ref.at[pl.ds(kept_at, half)], kept_ref, sem.at[2]),
    ]
    for copy in copies:
        copy.start()
    copies[0].wait()
    groups = starts_ref.shape[0]
    need_ref[0] = 0
    for g in range(groups):
        table_ref[g] = g
    if adaptive:
        starts = [raw_ref[g] for g in range(groups)]
        reach = []
        for start in starts:
            low = start // chip_tokens
            high = (start + (R_DEV - 1)) // chip_tokens
            reach.append(
                [
                    jnp.left_shift(1, jnp.bitwise_xor(low, h))
                    | jnp.left_shift(1, jnp.bitwise_xor(high, h))
                    for h in range(groups)
                ]
            )
        best = cost = homes = None
        for order in itertools.permutations(range(groups)):
            mask = functools.reduce(
                jnp.bitwise_or, [reach[w][h] for h, w in enumerate(order)]
            )
            price = sum((jnp.right_shift(mask, k) & 1) * (4 if k == 1 else 5) for k in range(1, groups))
            packed = jnp.int32(sum(w << (4 * h) for h, w in enumerate(order)))
            if best is None:
                best, cost, homes = mask, price, packed
            else:
                better = price < cost
                best = jnp.where(better, mask, best)
                homes = jnp.where(better, packed, homes)
                cost = jnp.where(better, price, cost)
        need_ref[0] = jnp.right_shift(best, 1)
        for h in range(groups):
            table_ref[h] = jnp.right_shift(homes, 4 * h) & 15
    for g in range(groups):
        table_ref[groups + g] = raw_ref[table_ref[g]]
    for copy in copies[1:]:
        copy.wait()


def prep_kernel(*refs):
    sources, outs, scratch = refs[:8], refs[8:14], refs[14:]
    wbd_ref, bias_ref = outs[:2]
    w_ref, tri_ref, chain_ref, off_ref, sem = scratch
    targets = [w_ref, tri_ref, chain_ref, off_ref, *outs[2:]]
    copies = [
        pltpu.make_async_copy(a, b, sem.at[n])
        for n, (a, b) in enumerate(zip(sources, targets))
    ]
    for copy in copies:
        copy.start()
    wbd_ref[...] = jnp.zeros_like(wbd_ref)
    for copy in copies:
        copy.wait()
    for c in range(PROJ_CHANNELS):
        block = w_ref[c * PROJ_CHANNELS : (c + 1) * PROJ_CHANNELS, :]
        for j in range(PACK):
            row = c * LANES + j * PROJ_CHANNELS
            wbd_ref[row : row + PROJ_CHANNELS, j * CZ : (j + 1) * CZ] = block
    tokens, keys = tri_ref.shape[1:]
    first = lax.axis_index("res") * tokens
    chain = jnp.broadcast_to(chain_ref[...], (tokens, keys))
    rows = lax.broadcasted_iota(jnp.int32, (tokens, keys), 0)
    cols = lax.broadcasted_iota(jnp.int32, (tokens, keys), 1)
    own = jnp.sum(jnp.where(cols == rows + first, chain, 0), axis=1, keepdims=True)
    differ = (chain != own).astype(F32)
    for h in range(H):
        bias_ref[h * tokens : (h + 1) * tokens, :] = (
            tri_ref[h].astype(F32) + off_ref[h] * differ
        )


def select_kernel(table, own_ref, recv_ref, *refs):
    outs, chip_ref = refs[:-1], refs[-1]
    chips = len(outs)
    size, _ = outs[0].shape
    width = own_ref.shape[1]
    res = lax.axis_index("res")
    core = res % 2
    z = res // 2
    own_at = pl.multiple_of(core * width, LANES)
    recv_at = pl.multiple_of((1 - core) * width, LANES)
    chip_ref[:, pl.ds(own_at, width)] = own_ref[...]
    chip_ref[:, pl.ds(recv_at, width)] = recv_ref[...]
    m = lax.broadcasted_iota(jnp.int32, (size, SPAN), 0)
    lane = lax.broadcasted_iota(jnp.int32, (size, SPAN), 1)
    delta = lane - (m % R_DEV) * PROJ_CHANNELS - m // R_DEV
    split = WINDOW // size
    groups = chips // split
    for k in range(chips):
        at = jnp.bitwise_xor(z, k)
        first = at % split * (size // R_DEV)
        start = table[groups + at // split] * PROJ_CHANNELS - z * (2 * width)
        base = jnp.clip(start, 0, 2 * width - SPAN) // LANES * LANES
        base = pl.multiple_of(base, LANES)
        pick = (delta == start + first - base).astype(F32).astype(BF)
        outs[k][...] = lax.dot_general(
            pick,
            chip_ref[:, pl.ds(base, SPAN)],
            (((1,), (1,)), ((), ())),
            preferred_element_type=F32,
        ).astype(BF)


def outer_kernel(chips, table, *refs):
    mine, theirs = refs[:chips], refs[chips : 2 * chips]
    b_ref, wbd_ref, *outs = refs[2 * chips : -3]
    at_ref, lhs_ref, acc_ref = refs[-3:]
    size, half = mine[0].shape
    groups = len(outs)
    z = lax.axis_index("res") // 2
    core = lax.axis_index("res") % 2
    mine_at = pl.multiple_of(core * half, LANES)
    theirs_at = pl.multiple_of((1 - core) * half, LANES)
    for k in range(chips):
        at = jnp.bitwise_xor(z, k)
        split = WINDOW // size
        row = pl.multiple_of(table[at // split] * WINDOW + at % split * size, size)
        at_ref[pl.ds(row, size), pl.ds(mine_at, half)] = mine[k][...]
        at_ref[pl.ds(row, size), pl.ds(theirs_at, half)] = theirs[k][...]
    width = b_ref.shape[1]
    rows = groups * R_DEV
    for n in range(width // (2 * LANES)):
        part = jnp.dot(
            at_ref[...],
            b_ref[:, n * 2 * LANES : (n + 1) * 2 * LANES],
            preferred_element_type=F32,
        ).reshape(groups, PROJ_CHANNELS, R_DEV, 2 * LANES)
        for c in range(PROJ_CHANNELS):
            for q in range(2):
                slab = part[:, c, :, q * LANES : (q + 1) * LANES].reshape(rows, LANES)
                lhs_ref[
                    (2 * n + q) * rows : (2 * n + q + 1) * rows,
                    c * LANES : (c + 1) * LANES,
                ] = slab.astype(BF)
    acc = jnp.dot(lhs_ref[...], wbd_ref[...], preferred_element_type=F32)
    chunks = width // LANES
    acc_ref[...] = acc.reshape(chunks, groups, R_DEV, PACK * CZ)
    for k in range(groups):
        g = jnp.bitwise_xor(lax.axis_index("depth"), k)
        block = acc_ref[:, g]
        block = jnp.stack(
            [block[:, :, j * CZ : (j + 1) * CZ] for j in range(PACK)], axis=1
        )
        outs[k][...] = block.reshape(chunks * PACK * R_DEV, CZ).astype(BF)


def norm_kernel(scale, *refs):
    parts = refs[:-4]
    bias_ref, pair_ref, normed_ref, sum_ref = refs[-4:]
    total = parts[0][...].astype(F32)
    for p in parts[1:]:
        total = total + p[...].astype(F32)
    sum_ref[...] = total * scale + bias_ref[...]
    tokens = pair_ref.shape[1]
    for u in range(R_DEV):
        pair = sum_ref[pl.ds(u, tokens, stride=R_DEV), :].astype(BF)
        pair_ref[u] = pair
        values = pair.astype(F32)
        centred = values - jnp.mean(values, axis=-1, keepdims=True)
        variance = jnp.mean(centred * centred, axis=-1, keepdims=True)
        normed_ref[u] = (centred * lax.rsqrt(variance + epsilon)).astype(BF)


def query_kernel(normed_ref, w_ref, q_ref, gate_ref):
    rows = R_DEV * normed_ref.shape[1]
    x = normed_ref[...].reshape(rows, CZ)
    q_ref[...] = jnp.dot(x, w_ref[:, :CZ], preferred_element_type=F32).astype(BF)
    g = jnp.dot(x, w_ref[:, 3 * CZ :], preferred_element_type=F32).astype(BF)
    gate_ref[...] = jax.nn.sigmoid(g.astype(F32))


def attend_kernel(chips, *refs):
    mine, theirs = refs[:chips], refs[chips : 2 * chips]
    q_ref, gate_ref, w_ref, wo_ref, bias_ref, out_ref = refs[2 * chips : -4]
    all_ref, kv_ref, scores_ref, gated_ref = refs[-4:]
    tokens = mine[0].shape[1]
    z = lax.axis_index("res") // 2
    core = lax.axis_index("res") % 2
    for k in range(chips):
        chip = jnp.bitwise_xor(z, k) * 2
        mine_at = pl.multiple_of((chip + core) * tokens, tokens)
        theirs_at = pl.multiple_of((chip + 1 - core) * tokens, tokens)
        all_ref[:, pl.ds(mine_at, tokens), :] = mine[k][...]
        all_ref[:, pl.ds(theirs_at, tokens), :] = theirs[k][...]
    scale = DH ** (-0.5)
    lane_head = lax.broadcasted_iota(jnp.int32, (tokens, CZ), 1) // DH
    kv = jnp.dot(
        all_ref[...].reshape(-1, CZ), w_ref[:, CZ : 3 * CZ], preferred_element_type=F32
    )
    kv_ref[...] = kv.astype(BF).reshape(kv_ref.shape)
    for u in range(R_DEV):
        q = q_ref[u * tokens : (u + 1) * tokens, :]
        spread = jnp.concatenate(
            [jnp.where(lane_head == h, q, jnp.zeros_like(q)) for h in range(H)], axis=0
        )
        scores = lax.dot_general(
            spread, kv_ref[u, :, :CZ], (((1,), (1,)), ((), ())), preferred_element_type=F32
        )
        scores_ref[u] = scores * scale + bias_ref[...]
    for u in range(R_DEV):
        scores = scores_ref[u]
        weights = jnp.exp(scores - jnp.max(scores, axis=-1, keepdims=True))
        denom = jnp.sum(weights, axis=-1, keepdims=True)
        value = jnp.dot(
            weights.astype(BF), kv_ref[u, :, CZ:], preferred_element_type=F32
        )
        value = value / denom
        attended = jnp.zeros((tokens, CZ), F32)
        for h in range(H):
            attended = jnp.where(
                lane_head == h, value[h * tokens : (h + 1) * tokens, :], attended
            )
        gated_ref[u * tokens : (u + 1) * tokens, :] = (
            gate_ref[u * tokens : (u + 1) * tokens, :] * attended
        ).astype(BF)
    out = jnp.dot(gated_ref[...], wo_ref[...], preferred_element_type=F32)
    out_ref[...] = out.astype(BF).reshape(R_DEV, tokens, CZ)


def in_hbm(*arrays):
    return [pltpu.with_memory_space_constraint(a, pltpu.HBM) for a in arrays]


def swap(x, axis, mask):
    n = lax.axis_size(axis)
    return lax.ppermute(x, axis, [(i, i ^ mask) for i in range(n)])


def body(
    alignment_left,
    alignment_right,
    window_starts,
    outer_product_weight,
    outer_product_bias,
    query_key_value_gate_weight,
    output_weight,
    triangle_pair_bias,
    residue_chain,
    interchain_offset,
):
    depth_count = lax.axis_size("depth")
    res_count = lax.axis_size("res")
    groups = window_starts.shape[0]
    chips = res_count // 2
    size = groups * WINDOW // chips
    assert groups == depth_count and WINDOW % size == 0
    seqs, width = alignment_left.shape
    half = seqs // 2
    tokens = width // PROJ_CHANNELS
    keys = residue_chain.shape[0]
    rows = groups * R_DEV

    adaptive = chips == groups == 4
    sent, kept, table, need = call(
        functools.partial(front_kernel, adaptive, 2 * tokens),
        [
            pltpu.VMEM((half, width), BF),
            pltpu.VMEM((half, width), BF),
            pltpu.SMEM((2 * groups,), jnp.int32),
            pltpu.SMEM((1,), jnp.int32),
        ],
        [ANY, ANY],
        [pltpu.SMEM(window_starts.shape, jnp.int32), pltpu.SemaphoreType.DMA((3,))],
    )(*in_hbm(alignment_left, window_starts))
    recv = swap(sent, "res", 1)

    wbd, bias, right, qkvg, wo, shift = call(
        prep_kernel,
        [
            pltpu.VMEM((PROJ_CHANNELS * LANES, PACK * CZ), BF),
            pltpu.VMEM((H * tokens, keys), F32),
            pltpu.VMEM(alignment_right.shape, BF),
            pltpu.VMEM(query_key_value_gate_weight.shape, BF),
            pltpu.VMEM(output_weight.shape, BF),
            pltpu.VMEM((1, CZ), F32),
        ],
        [ANY] * 8,
        [
            pltpu.VMEM(outer_product_weight.shape, BF),
            pltpu.VMEM(triangle_pair_bias.shape, BF),
            pltpu.VMEM((1, keys), jnp.int32),
            pltpu.SMEM((H,), F32),
            pltpu.SemaphoreType.DMA((8,)),
        ],
        flops=1 << 28,
    )(
        *in_hbm(
            outer_product_weight,
            triangle_pair_bias,
            residue_chain[None, :],
            interchain_offset,
            alignment_right,
            query_key_value_gate_weight,
            output_weight,
            outer_product_bias[None, :],
        )
    )

    picked = call(
        select_kernel,
        [pltpu.VMEM((size, half), BF)] * chips,
        [SMEM, VMEM, VMEM],
        [pltpu.VMEM((half, 2 * width), BF)],
        flops=1 << 28,
    )(table, kept, recv)

    def collect(wanted, *picked):
        return functools.reduce(
            jnp.add,
            [picked[0]] + [swap(picked[k], "res", 2 * k) for k in wanted],
        )

    every = range(1, chips)
    if adaptive:
        subsets = [
            [k for k in every if bits >> (k - 1) & 1] for bits in range(1 << len(every))
        ]
        piece = lax.switch(
            need[0], [functools.partial(collect, wanted) for wanted in subsets], *picked
        )
    else:
        piece = collect(every, *picked)
    mine = [piece] + [swap(piece, "res", 2 * k) for k in range(1, chips)]
    theirs = [swap(m, "res", 1) for m in mine]

    partial = call(
        functools.partial(outer_kernel, chips),
        [pltpu.VMEM((R_DEV * tokens, CZ), BF)] * groups,
        [SMEM] + [VMEM] * (2 * chips + 2),
        [
            pltpu.VMEM((groups * WINDOW, seqs), BF),
            pltpu.VMEM((rows * width // LANES, PROJ_CHANNELS * LANES), BF),
            pltpu.VMEM((width // LANES, groups, R_DEV, PACK * CZ), F32),
        ],
        flops=1 << 31,
        limit=32,
    )(table, *mine, *theirs, right, wbd)
    parts = [partial[0]] + [swap(partial[k], "depth", k) for k in range(1, groups)]

    pair_strip, normed = call(
        functools.partial(norm_kernel, 1.0 / (seqs * depth_count)),
        [
            jax.ShapeDtypeStruct((R_DEV, tokens, CZ), BF),
            pltpu.VMEM((R_DEV, tokens, CZ), BF),
        ],
        [VMEM] * (groups + 1),
        [pltpu.VMEM((R_DEV * tokens, CZ), F32)],
        flops=1 << 24,
    )(*parts, shift)

    near = [normed] + [swap(normed, "res", 2 * k) for k in range(1, chips)]
    far = [swap(n, "res", 1) for n in near]
    queries, gate = call(
        query_kernel,
        [
            pltpu.VMEM((R_DEV * tokens, CZ), BF),
            pltpu.VMEM((R_DEV * tokens, CZ), F32),
        ],
        [VMEM] * 2,
        flops=1 << 27,
    )(normed, qkvg)
    (update,) = call(
        functools.partial(attend_kernel, chips),
        [jax.ShapeDtypeStruct((R_DEV, tokens, CZ), BF)],
        [VMEM] * (2 * chips + 5),
        [
            pltpu.VMEM((R_DEV, keys, CZ), BF),
            pltpu.VMEM((R_DEV, keys, 2 * CZ), BF),
            pltpu.VMEM((R_DEV, H * tokens, keys), F32),
            pltpu.VMEM((R_DEV * tokens, CZ), BF),
        ],
        flops=1 << 29,
        limit=24,
    )(*near, *far, queries, gate, qkvg, wo, bias)
    return (pair_strip, update)


def solution(mesh):
    in_specs = (
        P("depth", "res"),
        P("depth", "res"),
        P(),
        P(),
        P(),
        P(),
        P(),
        P(None, "res", None),
        P(),
        P(),
    )
    out_specs = (P("depth", "res", None), P("depth", "res", None))
    return jax.shard_map(body, mesh=mesh, in_specs=in_specs, out_specs=out_specs, check_vma=False)
```

```python
import functools
import itertools

import jax
import jax.numpy as jnp
from jax import lax
from jax.experimental import pallas as pl
from jax.experimental.pallas import tpu as pltpu
from jax.sharding import PartitionSpec as P


PROJ_CHANNELS = 32
CZ = 128
H = 4
DH = 32
R_DEV = 8
LANES = 128
PACK = LANES // PROJ_CHANNELS
WINDOW = R_DEV * PROJ_CHANNELS
SPAN = WINDOW + LANES


epsilon = 1e-05
VMEM = pl.BlockSpec(memory_space=pltpu.VMEM)
SMEM = pl.BlockSpec(memory_space=pltpu.SMEM)
ANY = pl.BlockSpec(memory_space=pltpu.HBM)
BF = jnp.bfloat16
F32 = jnp.float32


def call(kernel, outs, specs, scratch=(), flops=0, limit=8):
    return pl.pallas_call(
        kernel,
        out_shape=outs,
        in_specs=specs,
        out_specs=[
            SMEM if getattr(o, "memory_space", None) == pltpu.SMEM else VMEM for o in outs
        ],
        scratch_shapes=list(scratch),
        compiler_params=pltpu.CompilerParams(vmem_limit_bytes=limit << 20),
        cost_estimate=pl.CostEstimate(
            flops=flops, bytes_accessed=1 << 20, transcendentals=0
        ),
    )


INNER, FAR = 16, 32


def near_price(mask):
    one, inner, far = (jnp.right_shift(mask, n) & 1 for n in (1, 4, 5))
    return one * 5 + inner * 6 + far * 100


def swap_price(mask):
    one, two, three = (jnp.right_shift(mask, n) & 1 for n in (1, 2, 3))
    return one * 5 + two * 12 + three * 10


def front_kernel(adaptive, chip_tokens, left_ref, starts_ref, sent_ref, kept_ref, table_ref, need_ref, raw_ref, sem):
    half = sent_ref.shape[0]
    core = lax.axis_index("res") % 2
    sent_at = pl.multiple_of((1 - core) * half, half)
    kept_at = pl.multiple_of(core * half, half)
    copies = [
        pltpu.make_async_copy(starts_ref, raw_ref, sem.at[0]),
        pltpu.make_async_copy(left_ref.at[pl.ds(sent_at, half)], sent_ref, sem.at[1]),
        pltpu.make_async_copy(left_ref.at[pl.ds(kept_at, half)], kept_ref, sem.at[2]),
    ]
    for copy in copies:
        copy.start()
    copies[0].wait()
    groups = starts_ref.shape[0]
    need_ref[0] = 0
    for g in range(groups):
        table_ref[g] = g
    if adaptive:
        starts = [raw_ref[g] for g in range(groups)]
        reach = []
        for start in starts:
            ends = [start // chip_tokens, (start + (R_DEV - 1)) // chip_tokens]
            reach.append([])
            for h in range(groups):
                bits = 0
                for end in ends:
                    step = jnp.abs(h - end)
                    swap_bits = jnp.bitwise_xor(end, h)
                    bits |= jnp.left_shift(1, swap_bits)
                    bits |= jnp.where((swap_bits == 3) & (step == 1), INNER, 0)
                    bits |= jnp.where(step > 1, FAR, 0)
                reach[-1].append(bits)
        best = cost = homes = None
        for order in itertools.permutations(range(groups)):
            mask = functools.reduce(
                jnp.bitwise_or, [reach[w][h] for h, w in enumerate(order)]
            )
            price = jnp.minimum(near_price(mask), swap_price(mask))
            packed = jnp.int32(sum(w << (4 * h) for h, w in enumerate(order)))
            if best is None:
                best, cost, homes = mask, price, packed
            else:
                better = price < cost
                best = jnp.where(better, mask, best)
                homes = jnp.where(better, packed, homes)
                cost = jnp.where(better, price, cost)
        inner = (best & INNER) > 0
        near = inner & (near_price(best) <= swap_price(best))
        one = jnp.right_shift(best, 1) & 1
        need_ref[0] = jnp.where(near, 8 + one, jnp.right_shift(best, 1) & 7)
        for h in range(groups):
            table_ref[h] = jnp.right_shift(homes, 4 * h) & 15
    for g in range(groups):
        table_ref[groups + g] = raw_ref[table_ref[g]]
    for copy in copies[1:]:
        copy.wait()


def prep_kernel(*refs):
    sources, outs, scratch = refs[:8], refs[8:14], refs[14:]
    wbd_ref, bias_ref = outs[:2]
    w_ref, tri_ref, chain_ref, off_ref, sem = scratch
    targets = [w_ref, tri_ref, chain_ref, off_ref, *outs[2:]]
    copies = [
        pltpu.make_async_copy(a, b, sem.at[n])
        for n, (a, b) in enumerate(zip(sources, targets))
    ]
    for copy in copies:
        copy.start()
    wbd_ref[...] = jnp.zeros_like(wbd_ref)
    for copy in copies:
        copy.wait()
    for c in range(PROJ_CHANNELS):
        block = w_ref[c * PROJ_CHANNELS : (c + 1) * PROJ_CHANNELS, :]
        for j in range(PACK):
            row = c * LANES + j * PROJ_CHANNELS
            wbd_ref[row : row + PROJ_CHANNELS, j * CZ : (j + 1) * CZ] = block
    tokens, keys = tri_ref.shape[1:]
    first = lax.axis_index("res") * tokens
    chain = jnp.broadcast_to(chain_ref[...], (tokens, keys))
    rows = lax.broadcasted_iota(jnp.int32, (tokens, keys), 0)
    cols = lax.broadcasted_iota(jnp.int32, (tokens, keys), 1)
    own = jnp.sum(jnp.where(cols == rows + first, chain, 0), axis=1, keepdims=True)
    differ = (chain != own).astype(F32)
    for h in range(H):
        bias_ref[h * tokens : (h + 1) * tokens, :] = (
            tri_ref[h].astype(F32) + off_ref[h] * differ
        )


def select_kernel(table, own_ref, recv_ref, *refs):
    outs, chip_ref = refs[:-1], refs[-1]
    chips = len(outs)
    size, _ = outs[0].shape
    width = own_ref.shape[1]
    res = lax.axis_index("res")
    core = res % 2
    z = res // 2
    own_at = pl.multiple_of(core * width, LANES)
    recv_at = pl.multiple_of((1 - core) * width, LANES)
    chip_ref[:, pl.ds(own_at, width)] = own_ref[...]
    chip_ref[:, pl.ds(recv_at, width)] = recv_ref[...]
    m = lax.broadcasted_iota(jnp.int32, (size, SPAN), 0)
    lane = lax.broadcasted_iota(jnp.int32, (size, SPAN), 1)
    delta = lane - (m % R_DEV) * PROJ_CHANNELS - m // R_DEV
    split = WINDOW // size
    groups = chips // split
    for k in range(chips):
        at = jnp.bitwise_xor(z, k)
        first = at % split * (size // R_DEV)
        start = table[groups + at // split] * PROJ_CHANNELS - z * (2 * width)
        base = jnp.clip(start, 0, 2 * width - SPAN) // LANES * LANES
        base = pl.multiple_of(base, LANES)
        pick = (delta == start + first - base).astype(F32).astype(BF)
        outs[k][...] = lax.dot_general(
            pick,
            chip_ref[:, pl.ds(base, SPAN)],
            (((1,), (1,)), ((), ())),
            preferred_element_type=F32,
        ).astype(BF)


def outer_kernel(chips, table, *refs):
    mine, theirs = refs[:chips], refs[chips : 2 * chips]
    b_ref, wbd_ref, *outs = refs[2 * chips : -3]
    at_ref, lhs_ref, acc_ref = refs[-3:]
    size, half = mine[0].shape
    groups = len(outs)
    z = lax.axis_index("res") // 2
    core = lax.axis_index("res") % 2
    mine_at = pl.multiple_of(core * half, LANES)
    theirs_at = pl.multiple_of((1 - core) * half, LANES)
    for k in range(chips):
        at = jnp.bitwise_xor(z, k)
        split = WINDOW // size
        row = pl.multiple_of(table[at // split] * WINDOW + at % split * size, size)
        at_ref[pl.ds(row, size), pl.ds(mine_at, half)] = mine[k][...]
        at_ref[pl.ds(row, size), pl.ds(theirs_at, half)] = theirs[k][...]
    width = b_ref.shape[1]
    rows = groups * R_DEV
    for n in range(width // (2 * LANES)):
        part = jnp.dot(
            at_ref[...],
            b_ref[:, n * 2 * LANES : (n + 1) * 2 * LANES],
            preferred_element_type=F32,
        ).reshape(groups, PROJ_CHANNELS, R_DEV, 2 * LANES)
        for c in range(PROJ_CHANNELS):
            for q in range(2):
                slab = part[:, c, :, q * LANES : (q + 1) * LANES].reshape(rows, LANES)
                lhs_ref[
                    (2 * n + q) * rows : (2 * n + q + 1) * rows,
                    c * LANES : (c + 1) * LANES,
                ] = slab.astype(BF)
    acc = jnp.dot(lhs_ref[...], wbd_ref[...], preferred_element_type=F32)
    chunks = width // LANES
    acc_ref[...] = acc.reshape(chunks, groups, R_DEV, PACK * CZ)
    for k in range(groups):
        g = jnp.bitwise_xor(lax.axis_index("depth"), k)
        block = acc_ref[:, g]
        block = jnp.stack(
            [block[:, :, j * CZ : (j + 1) * CZ] for j in range(PACK)], axis=1
        )
        outs[k][...] = block.reshape(chunks * PACK * R_DEV, CZ).astype(BF)


def norm_kernel(scale, *refs):
    parts = refs[:-4]
    bias_ref, pair_ref, normed_ref, sum_ref = refs[-4:]
    total = parts[0][...].astype(F32)
    for p in parts[1:]:
        total = total + p[...].astype(F32)
    sum_ref[...] = total * scale + bias_ref[...]
    tokens = pair_ref.shape[1]
    for u in range(R_DEV):
        pair = sum_ref[pl.ds(u, tokens, stride=R_DEV), :].astype(BF)
        pair_ref[u] = pair
        values = pair.astype(F32)
        centred = values - jnp.mean(values, axis=-1, keepdims=True)
        variance = jnp.mean(centred * centred, axis=-1, keepdims=True)
        normed_ref[u] = (centred * lax.rsqrt(variance + epsilon)).astype(BF)


def query_kernel(normed_ref, w_ref, pair_ref, q_ref, gate_ref, strip_ref):
    strip_ref[...] = pair_ref[...]
    rows = R_DEV * normed_ref.shape[1]
    x = normed_ref[...].reshape(rows, CZ)
    q_ref[...] = jnp.dot(x, w_ref[:, :CZ], preferred_element_type=F32).astype(BF)
    g = jnp.dot(x, w_ref[:, 3 * CZ :], preferred_element_type=F32).astype(BF)
    gate_ref[...] = jax.nn.sigmoid(g.astype(F32))


def attend_kernel(chips, *refs):
    mine, theirs = refs[:chips], refs[chips : 2 * chips]
    q_ref, gate_ref, w_ref, wo_ref, bias_ref, out_ref = refs[2 * chips : -4]
    all_ref, kv_ref, scores_ref, gated_ref = refs[-4:]
    tokens = mine[0].shape[1]
    z = lax.axis_index("res") // 2
    core = lax.axis_index("res") % 2
    for k in range(chips):
        chip = jnp.bitwise_xor(z, k) * 2
        mine_at = pl.multiple_of((chip + core) * tokens, tokens)
        theirs_at = pl.multiple_of((chip + 1 - core) * tokens, tokens)
        all_ref[:, pl.ds(mine_at, tokens), :] = mine[k][...]
        all_ref[:, pl.ds(theirs_at, tokens), :] = theirs[k][...]
    scale = DH ** (-0.5)
    lane_head = lax.broadcasted_iota(jnp.int32, (tokens, CZ), 1) // DH
    kv = jnp.dot(
        all_ref[...].reshape(-1, CZ), w_ref[:, CZ : 3 * CZ], preferred_element_type=F32
    )
    kv_ref[...] = kv.astype(BF).reshape(kv_ref.shape)
    for u in range(R_DEV):
        q = q_ref[u * tokens : (u + 1) * tokens, :]
        spread = jnp.concatenate(
            [jnp.where(lane_head == h, q, jnp.zeros_like(q)) for h in range(H)], axis=0
        )
        scores = lax.dot_general(
            spread, kv_ref[u, :, :CZ], (((1,), (1,)), ((), ())), preferred_element_type=F32
        )
        scores_ref[u] = scores * scale + bias_ref[...]
    for u in range(R_DEV):
        scores = scores_ref[u]
        weights = jnp.exp(scores - jnp.max(scores, axis=-1, keepdims=True))
        denom = jnp.sum(weights, axis=-1, keepdims=True)
        value = jnp.dot(
            weights.astype(BF), kv_ref[u, :, CZ:], preferred_element_type=F32
        )
        value = value / denom
        attended = jnp.zeros((tokens, CZ), F32)
        for h in range(H):
            attended = jnp.where(
                lane_head == h, value[h * tokens : (h + 1) * tokens, :], attended
            )
        gated_ref[u * tokens : (u + 1) * tokens, :] = (
            gate_ref[u * tokens : (u + 1) * tokens, :] * attended
        ).astype(BF)
    out = jnp.dot(gated_ref[...], wo_ref[...], preferred_element_type=F32)
    out_ref[...] = out.astype(BF).reshape(R_DEV, tokens, CZ)


def in_hbm(*arrays):
    return [pltpu.with_memory_space_constraint(a, pltpu.HBM) for a in arrays]


def swap(x, axis, mask):
    n = lax.axis_size(axis)
    return lax.ppermute(x, axis, [(i, i ^ mask) for i in range(n)])


def body(
    alignment_left,
    alignment_right,
    window_starts,
    outer_product_weight,
    outer_product_bias,
    query_key_value_gate_weight,
    output_weight,
    triangle_pair_bias,
    residue_chain,
    interchain_offset,
):
    depth_count = lax.axis_size("depth")
    res_count = lax.axis_size("res")
    groups = window_starts.shape[0]
    chips = res_count // 2
    size = groups * WINDOW // chips
    assert groups == depth_count and WINDOW % size == 0
    seqs, width = alignment_left.shape
    half = seqs // 2
    tokens = width // PROJ_CHANNELS
    keys = residue_chain.shape[0]
    rows = groups * R_DEV

    adaptive = chips == groups == 4
    sent, kept, table, need = call(
        functools.partial(front_kernel, adaptive, 2 * tokens),
        [
            pltpu.VMEM((half, width), BF),
            pltpu.VMEM((half, width), BF),
            pltpu.SMEM((2 * groups,), jnp.int32),
            pltpu.SMEM((1,), jnp.int32),
        ],
        [ANY, ANY],
        [pltpu.SMEM(window_starts.shape, jnp.int32), pltpu.SemaphoreType.DMA((3,))],
    )(*in_hbm(alignment_left, window_starts))
    recv = swap(sent, "res", 1)

    wbd, bias, right, qkvg, wo, shift = call(
        prep_kernel,
        [
            pltpu.VMEM((PROJ_CHANNELS * LANES, PACK * CZ), BF),
            pltpu.VMEM((H * tokens, keys), F32),
            pltpu.VMEM(alignment_right.shape, BF),
            pltpu.VMEM(query_key_value_gate_weight.shape, BF),
            pltpu.VMEM(output_weight.shape, BF),
            pltpu.VMEM((1, CZ), F32),
        ],
        [ANY] * 8,
        [
            pltpu.VMEM(outer_product_weight.shape, BF),
            pltpu.VMEM(triangle_pair_bias.shape, BF),
            pltpu.VMEM((1, keys), jnp.int32),
            pltpu.SMEM((H,), F32),
            pltpu.SemaphoreType.DMA((8,)),
        ],
        flops=1 << 28,
    )(
        *in_hbm(
            outer_product_weight,
            triangle_pair_bias,
            residue_chain[None, :],
            interchain_offset,
            alignment_right,
            query_key_value_gate_weight,
            output_weight,
            outer_product_bias[None, :],
        )
    )

    picked = call(
        select_kernel,
        [pltpu.VMEM((size, half), BF)] * chips,
        [SMEM, VMEM, VMEM],
        [pltpu.VMEM((half, 2 * width), BF)],
        flops=1 << 28,
    )(table, kept, recv)

    def collect(wanted, *picked):
        return functools.reduce(
            jnp.add,
            [picked[0]] + [swap(picked[k], "res", 2 * k) for k in wanted],
        )

    def collect_near(one, *picked):
        inner = [r for r in range(res_count) if abs(r // 2 - (r ^ 6) // 2) == 1]
        pairs = [(r, r ^ 6 if r in inner else r ^ 1) for r in range(res_count)]
        moved = [picked[0], lax.ppermute(picked[3], "res", pairs)]
        if one:
            moved.append(swap(picked[1], "res", 2))
        return functools.reduce(jnp.add, moved)

    every = range(1, chips)
    if adaptive:
        subsets = [
            [k for k in every if bits >> (k - 1) & 1] for bits in range(1 << len(every))
        ]
        branches = [functools.partial(collect, wanted) for wanted in subsets]
        branches += [functools.partial(collect_near, one) for one in (False, True)]
        piece = lax.switch(need[0], branches, *picked)
    else:
        piece = collect(every, *picked)
    mine = [piece] + [swap(piece, "res", 2 * k) for k in range(1, chips)]
    theirs = [swap(m, "res", 1) for m in mine]

    partial = call(
        functools.partial(outer_kernel, chips),
        [pltpu.VMEM((R_DEV * tokens, CZ), BF)] * groups,
        [SMEM] + [VMEM] * (2 * chips + 2),
        [
            pltpu.VMEM((groups * WINDOW, seqs), BF),
            pltpu.VMEM((rows * width // LANES, PROJ_CHANNELS * LANES), BF),
            pltpu.VMEM((width // LANES, groups, R_DEV, PACK * CZ), F32),
        ],
        flops=1 << 31,
        limit=32,
    )(table, *mine, *theirs, right, wbd)
    parts = [partial[0]] + [swap(partial[k], "depth", k) for k in range(1, groups)]

    pair, normed = call(
        functools.partial(norm_kernel, 1.0 / (seqs * depth_count)),
        [pltpu.VMEM((R_DEV, tokens, CZ), BF)] * 2,
        [VMEM] * (groups + 1),
        [pltpu.VMEM((R_DEV * tokens, CZ), F32)],
        flops=1 << 24,
    )(*parts, shift)

    near = [normed] + [swap(normed, "res", 2 * k) for k in range(1, chips)]
    far = [swap(n, "res", 1) for n in near]
    queries, gate, pair_strip = call(
        query_kernel,
        [
            pltpu.VMEM((R_DEV * tokens, CZ), BF),
            pltpu.VMEM((R_DEV * tokens, CZ), F32),
            jax.ShapeDtypeStruct((R_DEV, tokens, CZ), BF),
        ],
        [VMEM] * 3,
        flops=1 << 27,
    )(normed, qkvg, pair)
    (update,) = call(
        functools.partial(attend_kernel, chips),
        [jax.ShapeDtypeStruct((R_DEV, tokens, CZ), BF)],
        [VMEM] * (2 * chips + 5),
        [
            pltpu.VMEM((R_DEV, keys, CZ), BF),
            pltpu.VMEM((R_DEV, keys, 2 * CZ), BF),
            pltpu.VMEM((R_DEV, H * tokens, keys), F32),
            pltpu.VMEM((R_DEV * tokens, CZ), BF),
        ],
        flops=1 << 29,
        limit=24,
    )(*near, *far, queries, gate, qkvg, wo, bias)
    return (pair_strip, update)


def solution(mesh):
    in_specs = (
        P("depth", "res"),
        P("depth", "res"),
        P(),
        P(),
        P(),
        P(),
        P(),
        P(None, "res", None),
        P(),
        P(),
    )
    out_specs = (P("depth", "res", None), P("depth", "res", None))
    return jax.shard_map(body, mesh=mesh, in_specs=in_specs, out_specs=out_specs, check_vma=False)
```

```python
import functools
import itertools

import jax
import jax.numpy as jnp
from jax import lax
from jax.experimental import pallas as pl
from jax.experimental.pallas import tpu as pltpu
from jax.sharding import PartitionSpec as P


PROJ_CHANNELS = 32
CZ = 128
H = 4
DH = 32
R_DEV = 8
LANES = 128
PACK = LANES // PROJ_CHANNELS
WINDOW = R_DEV * PROJ_CHANNELS
SPAN = WINDOW + LANES


epsilon = 1e-05
VMEM = pl.BlockSpec(memory_space=pltpu.VMEM)
SMEM = pl.BlockSpec(memory_space=pltpu.SMEM)
ANY = pl.BlockSpec(memory_space=pltpu.HBM)
BF = jnp.bfloat16
F32 = jnp.float32


def call(kernel, outs, specs, scratch=(), flops=0, limit=8, aliases=None):
    return pl.pallas_call(
        kernel,
        out_shape=outs,
        in_specs=specs,
        out_specs=[
            SMEM if getattr(o, "memory_space", None) == pltpu.SMEM else VMEM for o in outs
        ],
        scratch_shapes=list(scratch),
        input_output_aliases=aliases or {},
        compiler_params=pltpu.CompilerParams(vmem_limit_bytes=limit << 20),
        cost_estimate=pl.CostEstimate(
            flops=flops, bytes_accessed=1 << 20, transcendentals=0
        ),
    )


INNER, FAR = 16, 32


def near_price(mask):
    one, inner, far = (jnp.right_shift(mask, n) & 1 for n in (1, 4, 5))
    return one * 5 + inner * 6 + far * 100


def swap_price(mask):
    one, two, three = (jnp.right_shift(mask, n) & 1 for n in (1, 2, 3))
    return one * 5 + two * 12 + three * 10


def front_kernel(adaptive, chip_tokens, left_ref, starts_ref, kept_ref, table_ref, need_ref, raw_ref, sem):
    half = kept_ref.shape[0]
    core = lax.axis_index("res") % 2
    kept_at = pl.multiple_of(core * half, half)
    copies = [
        pltpu.make_async_copy(starts_ref, raw_ref, sem.at[0]),
        pltpu.make_async_copy(left_ref.at[pl.ds(kept_at, half)], kept_ref, sem.at[1]),
    ]
    for copy in copies:
        copy.start()
    copies[0].wait()
    groups = starts_ref.shape[0]
    need_ref[0] = 0
    for g in range(groups):
        table_ref[g] = g
    if adaptive:
        starts = [raw_ref[g] for g in range(groups)]
        reach = []
        for start in starts:
            ends = [start // chip_tokens, (start + (R_DEV - 1)) // chip_tokens]
            reach.append([])
            for h in range(groups):
                bits = 0
                for end in ends:
                    step = jnp.abs(h - end)
                    swap_bits = jnp.bitwise_xor(end, h)
                    bits |= jnp.left_shift(1, swap_bits)
                    bits |= jnp.where((swap_bits == 3) & (step == 1), INNER, 0)
                    bits |= jnp.where(step > 1, FAR, 0)
                reach[-1].append(bits)
        best = cost = homes = None
        for order in itertools.permutations(range(groups)):
            mask = functools.reduce(
                jnp.bitwise_or, [reach[w][h] for h, w in enumerate(order)]
            )
            price = jnp.minimum(near_price(mask), swap_price(mask))
            packed = jnp.int32(sum(w << (4 * h) for h, w in enumerate(order)))
            if best is None:
                best, cost, homes = mask, price, packed
            else:
                better = price < cost
                best = jnp.where(better, mask, best)
                homes = jnp.where(better, packed, homes)
                cost = jnp.where(better, price, cost)
        inner = (best & INNER) > 0
        near = inner & (near_price(best) <= swap_price(best))
        one = jnp.right_shift(best, 1) & 1
        need_ref[0] = jnp.where(near, 8 + one, jnp.right_shift(best, 1) & 7)
        for h in range(groups):
            table_ref[h] = jnp.right_shift(homes, 4 * h) & 15
    for g in range(groups):
        table_ref[groups + g] = raw_ref[table_ref[g]]
    for copy in copies[1:]:
        copy.wait()


def prep_kernel(*refs):
    sources, outs, scratch = refs[:8], refs[8:14], refs[14:]
    wbd_ref, bias_ref = outs[:2]
    w_ref, tri_ref, chain_ref, off_ref, sem = scratch
    targets = [w_ref, tri_ref, chain_ref, off_ref, *outs[2:]]
    copies = [
        pltpu.make_async_copy(a, b, sem.at[n])
        for n, (a, b) in enumerate(zip(sources, targets))
    ]
    for copy in copies:
        copy.start()
    wbd_ref[...] = jnp.zeros_like(wbd_ref)
    for copy in copies:
        copy.wait()
    for c in range(PROJ_CHANNELS):
        block = w_ref[c * PROJ_CHANNELS : (c + 1) * PROJ_CHANNELS, :]
        for j in range(PACK):
            row = c * LANES + j * PROJ_CHANNELS
            wbd_ref[row : row + PROJ_CHANNELS, j * CZ : (j + 1) * CZ] = block
    tokens, keys = tri_ref.shape[1:]
    first = lax.axis_index("res") * tokens
    chain = jnp.broadcast_to(chain_ref[...], (tokens, keys))
    rows = lax.broadcasted_iota(jnp.int32, (tokens, keys), 0)
    cols = lax.broadcasted_iota(jnp.int32, (tokens, keys), 1)
    own = jnp.sum(jnp.where(cols == rows + first, chain, 0), axis=1, keepdims=True)
    differ = (chain != own).astype(F32)
    for h in range(H):
        bias_ref[h * tokens : (h + 1) * tokens, :] = (
            tri_ref[h].astype(F32) + off_ref[h] * differ
        )


def select_kernel(table, own_ref, recv_ref, *refs):
    outs, chip_ref = refs[:-1], refs[-1]
    chips = len(outs)
    size, half = outs[0].shape
    width = own_ref.shape[1]
    res = lax.axis_index("res")
    core = res % 2
    z = res // 2
    own_at = pl.multiple_of(core * width, LANES)
    recv_at = pl.multiple_of((1 - core) * width, LANES)
    chip_ref[:, pl.ds(own_at, width)] = own_ref[...]
    chip_ref[:, pl.ds(recv_at, width)] = recv_ref[pl.ds(pl.multiple_of(core * half, half), half), :]
    m = lax.broadcasted_iota(jnp.int32, (size, SPAN), 0)
    lane = lax.broadcasted_iota(jnp.int32, (size, SPAN), 1)
    delta = lane - (m % R_DEV) * PROJ_CHANNELS - m // R_DEV
    split = WINDOW // size
    groups = chips // split
    for k in range(chips):
        at = jnp.bitwise_xor(z, k)
        first = at % split * (size // R_DEV)
        start = table[groups + at // split] * PROJ_CHANNELS - z * (2 * width)
        base = jnp.clip(start, 0, 2 * width - SPAN) // LANES * LANES
        base = pl.multiple_of(base, LANES)
        pick = (delta == start + first - base).astype(F32).astype(BF)
        outs[k][...] = lax.dot_general(
            pick,
            chip_ref[:, pl.ds(base, SPAN)],
            (((1,), (1,)), ((), ())),
            preferred_element_type=F32,
        ).astype(BF)


def outer_kernel(chips, table, *refs):
    mine, theirs = refs[:chips], refs[chips : 2 * chips]
    b_ref, wbd_ref, *outs = refs[2 * chips : -3]
    at_ref, lhs_ref, acc_ref = refs[-3:]
    size, half = mine[0].shape
    groups = len(outs)
    z = lax.axis_index("res") // 2
    core = lax.axis_index("res") % 2
    mine_at = pl.multiple_of(core * half, LANES)
    theirs_at = pl.multiple_of((1 - core) * half, LANES)
    for k in range(chips):
        at = jnp.bitwise_xor(z, k)
        split = WINDOW // size
        row = pl.multiple_of(table[at // split] * WINDOW + at % split * size, size)
        at_ref[pl.ds(row, size), pl.ds(mine_at, half)] = mine[k][...]
        at_ref[pl.ds(row, size), pl.ds(theirs_at, half)] = theirs[k][...]
    width = b_ref.shape[1]
    rows = groups * R_DEV
    for n in range(width // (2 * LANES)):
        part = jnp.dot(
            at_ref[...],
            b_ref[:, n * 2 * LANES : (n + 1) * 2 * LANES],
            preferred_element_type=F32,
        ).reshape(groups, PROJ_CHANNELS, R_DEV, 2 * LANES)
        for c in range(PROJ_CHANNELS):
            for q in range(2):
                slab = part[:, c, :, q * LANES : (q + 1) * LANES].reshape(rows, LANES)
                lhs_ref[
                    (2 * n + q) * rows : (2 * n + q + 1) * rows,
                    c * LANES : (c + 1) * LANES,
                ] = slab.astype(BF)
    acc = jnp.dot(lhs_ref[...], wbd_ref[...], preferred_element_type=F32)
    chunks = width // LANES
    acc_ref[...] = acc.reshape(chunks, groups, R_DEV, PACK * CZ)
    for k in range(groups):
        g = jnp.bitwise_xor(lax.axis_index("depth"), k)
        block = acc_ref[:, g]
        block = jnp.stack(
            [block[:, :, j * CZ : (j + 1) * CZ] for j in range(PACK)], axis=1
        )
        outs[k][...] = block.reshape(chunks * PACK * R_DEV, CZ).astype(BF)


def norm_kernel(scale, *refs):
    parts = refs[:-4]
    bias_ref, pair_ref, normed_ref, sum_ref = refs[-4:]
    total = parts[0][...].astype(F32)
    for p in parts[1:]:
        total = total + p[...].astype(F32)
    sum_ref[...] = total * scale + bias_ref[...]
    tokens = pair_ref.shape[1]
    for u in range(R_DEV):
        pair = sum_ref[pl.ds(u, tokens, stride=R_DEV), :].astype(BF)
        pair_ref[u] = pair
        values = pair.astype(F32)
        centred = values - jnp.mean(values, axis=-1, keepdims=True)
        variance = jnp.mean(centred * centred, axis=-1, keepdims=True)
        normed_ref[u] = (centred * lax.rsqrt(variance + epsilon)).astype(BF)


def query_kernel(normed_ref, w_ref, pair_ref, q_ref, gate_ref, strip_ref):
    strip_ref[...] = pair_ref[...]
    rows = R_DEV * normed_ref.shape[1]
    x = normed_ref[...].reshape(rows, CZ)
    q_ref[...] = jnp.dot(x, w_ref[:, :CZ], preferred_element_type=F32).astype(BF)
    g = jnp.dot(x, w_ref[:, 3 * CZ :], preferred_element_type=F32).astype(BF)
    gate_ref[...] = jax.nn.sigmoid(g.astype(F32))


def near_kernel(chips, *refs):
    near, w_ref, kv_ref = refs[:chips], refs[chips], refs[chips + 1]
    fill(near, w_ref, kv_ref, lax.axis_index("res") % 2)


def fill(pieces, w_ref, kv_ref, core):
    tokens = pieces[0].shape[1]
    z = lax.axis_index("res") // 2
    for k, piece in enumerate(pieces):
        at = (jnp.bitwise_xor(z, k) * 2 + core) * tokens
        kv = jnp.dot(
            piece[...].reshape(R_DEV * tokens, CZ),
            w_ref[:, CZ : 3 * CZ],
            preferred_element_type=F32,
        )
        kv_ref[:, pl.ds(pl.multiple_of(at, tokens), tokens), :] = kv.astype(BF).reshape(
            R_DEV, tokens, 2 * CZ
        )


def attend_kernel(chips, *refs):
    far = refs[:chips]
    _, q_ref, gate_ref, w_ref, wo_ref, bias_ref, out_ref, kv_ref = refs[chips:-2]
    scores_ref, gated_ref = refs[-2:]
    tokens = far[0].shape[1]
    fill(far, w_ref, kv_ref, 1 - lax.axis_index("res") % 2)
    scale = DH ** (-0.5)
    lane_head = lax.broadcasted_iota(jnp.int32, (tokens, CZ), 1) // DH
    for u in range(R_DEV):
        q = q_ref[u * tokens : (u + 1) * tokens, :]
        spread = jnp.concatenate(
            [jnp.where(lane_head == h, q, jnp.zeros_like(q)) for h in range(H)], axis=0
        )
        scores = lax.dot_general(
            spread, kv_ref[u, :, :CZ], (((1,), (1,)), ((), ())), preferred_element_type=F32
        )
        scores_ref[u] = scores * scale + bias_ref[...]
    for u in range(R_DEV):
        scores = scores_ref[u]
        weights = jnp.exp(scores - jnp.max(scores, axis=-1, keepdims=True))
        denom = jnp.sum(weights, axis=-1, keepdims=True)
        value = jnp.dot(
            weights.astype(BF), kv_ref[u, :, CZ:], preferred_element_type=F32
        )
        value = value / denom
        attended = jnp.zeros((tokens, CZ), F32)
        for h in range(H):
            attended = jnp.where(
                lane_head == h, value[h * tokens : (h + 1) * tokens, :], attended
            )
        gated_ref[u * tokens : (u + 1) * tokens, :] = (
            gate_ref[u * tokens : (u + 1) * tokens, :] * attended
        ).astype(BF)
    out = jnp.dot(gated_ref[...], wo_ref[...], preferred_element_type=F32)
    out_ref[...] = out.astype(BF).reshape(R_DEV, tokens, CZ)


def in_hbm(*arrays):
    return [pltpu.with_memory_space_constraint(a, pltpu.HBM) for a in arrays]


def swap(x, axis, mask):
    n = lax.axis_size(axis)
    return lax.ppermute(x, axis, [(i, i ^ mask) for i in range(n)])


def body(
    alignment_left,
    alignment_right,
    window_starts,
    outer_product_weight,
    outer_product_bias,
    query_key_value_gate_weight,
    output_weight,
    triangle_pair_bias,
    residue_chain,
    interchain_offset,
):
    depth_count = lax.axis_size("depth")
    res_count = lax.axis_size("res")
    groups = window_starts.shape[0]
    chips = res_count // 2
    size = groups * WINDOW // chips
    assert groups == depth_count and WINDOW % size == 0
    seqs, width = alignment_left.shape
    half = seqs // 2
    tokens = width // PROJ_CHANNELS
    keys = residue_chain.shape[0]
    rows = groups * R_DEV

    adaptive = chips == groups == 4
    kept, table, need = call(
        functools.partial(front_kernel, adaptive, 2 * tokens),
        [
            pltpu.VMEM((half, width), BF),
            pltpu.SMEM((2 * groups,), jnp.int32),
            pltpu.SMEM((1,), jnp.int32),
        ],
        [ANY, ANY],
        [pltpu.SMEM(window_starts.shape, jnp.int32), pltpu.SemaphoreType.DMA((2,))],
    )(*in_hbm(alignment_left, window_starts))
    recv = swap(alignment_left, "res", 1)

    wbd, bias, right, qkvg, wo, shift = call(
        prep_kernel,
        [
            pltpu.VMEM((PROJ_CHANNELS * LANES, PACK * CZ), BF),
            pltpu.VMEM((H * tokens, keys), F32),
            pltpu.VMEM(alignment_right.shape, BF),
            pltpu.VMEM(query_key_value_gate_weight.shape, BF),
            pltpu.VMEM(output_weight.shape, BF),
            pltpu.VMEM((1, CZ), F32),
        ],
        [ANY] * 8,
        [
            pltpu.VMEM(outer_product_weight.shape, BF),
            pltpu.VMEM(triangle_pair_bias.shape, BF),
            pltpu.VMEM((1, keys), jnp.int32),
            pltpu.SMEM((H,), F32),
            pltpu.SemaphoreType.DMA((8,)),
        ],
        flops=1 << 28,
    )(
        *in_hbm(
            outer_product_weight,
            triangle_pair_bias,
            residue_chain[None, :],
            interchain_offset,
            alignment_right,
            query_key_value_gate_weight,
            output_weight,
            outer_product_bias[None, :],
        )
    )

    picked = call(
        select_kernel,
        [pltpu.VMEM((size, half), BF)] * chips,
        [SMEM, VMEM, VMEM],
        [pltpu.VMEM((half, 2 * width), BF)],
        flops=1 << 28,
    )(table, kept, recv)

    def collect(wanted, *picked):
        return functools.reduce(
            jnp.add,
            [picked[0]] + [swap(picked[k], "res", 2 * k) for k in wanted],
        )

    def collect_near(one, *picked):
        inner = [r for r in range(res_count) if abs(r // 2 - (r ^ 6) // 2) == 1]
        pairs = [(r, r ^ 6 if r in inner else r ^ 1) for r in range(res_count)]
        moved = [picked[0], lax.ppermute(picked[3], "res", pairs)]
        if one:
            moved.append(swap(picked[1], "res", 2))
        return functools.reduce(jnp.add, moved)

    every = range(1, chips)
    if adaptive:
        subsets = [
            [k for k in every if bits >> (k - 1) & 1] for bits in range(1 << len(every))
        ]
        branches = [functools.partial(collect, wanted) for wanted in subsets]
        branches += [functools.partial(collect_near, one) for one in (False, True)]
        piece = lax.switch(need[0], branches, *picked)
    else:
        piece = collect(every, *picked)
    mine = [piece] + [swap(piece, "res", 2 * k) for k in range(1, chips)]
    theirs = [swap(m, "res", 1) for m in mine]

    partial = call(
        functools.partial(outer_kernel, chips),
        [pltpu.VMEM((R_DEV * tokens, CZ), BF)] * groups,
        [SMEM] + [VMEM] * (2 * chips + 2),
        [
            pltpu.VMEM((groups * WINDOW, seqs), BF),
            pltpu.VMEM((rows * width // LANES, PROJ_CHANNELS * LANES), BF),
            pltpu.VMEM((width // LANES, groups, R_DEV, PACK * CZ), F32),
        ],
        flops=1 << 31,
        limit=32,
    )(table, *mine, *theirs, right, wbd)
    parts = [partial[0]] + [swap(partial[k], "depth", k) for k in range(1, groups)]

    pair, normed = call(
        functools.partial(norm_kernel, 1.0 / (seqs * depth_count)),
        [pltpu.VMEM((R_DEV, tokens, CZ), BF)] * 2,
        [VMEM] * (groups + 1),
        [pltpu.VMEM((R_DEV * tokens, CZ), F32)],
        flops=1 << 24,
    )(*parts, shift)

    near = [normed] + [swap(normed, "res", 2 * k) for k in range(1, chips)]
    far = [swap(n, "res", 1) for n in near]
    queries, gate, pair_strip = call(
        query_kernel,
        [
            pltpu.VMEM((R_DEV * tokens, CZ), BF),
            pltpu.VMEM((R_DEV * tokens, CZ), F32),
            jax.ShapeDtypeStruct((R_DEV, tokens, CZ), BF),
        ],
        [VMEM] * 3,
        flops=1 << 27,
    )(normed, qkvg, pair)
    kv = pltpu.VMEM((R_DEV, keys, 2 * CZ), BF)
    (half_kv,) = call(
        functools.partial(near_kernel, chips), [kv], [VMEM] * (chips + 1), flops=1 << 28
    )(*near, qkvg)
    update, _ = call(
        functools.partial(attend_kernel, chips),
        [jax.ShapeDtypeStruct((R_DEV, tokens, CZ), BF), kv],
        [VMEM] * (chips + 6),
        [
            pltpu.VMEM((R_DEV, H * tokens, keys), F32),
            pltpu.VMEM((R_DEV * tokens, CZ), BF),
        ],
        flops=1 << 29,
        limit=24,
        aliases={chips: 1},
    )(*far, half_kv, queries, gate, qkvg, wo, bias)
    return (pair_strip, update)


def solution(mesh):
    in_specs = (
        P("depth", "res"),
        P("depth", "res"),
        P(),
        P(),
        P(),
        P(),
        P(),
        P(None, "res", None),
        P(),
        P(),
    )
    out_specs = (P("depth", "res", None), P("depth", "res", None))
    return jax.shard_map(body, mesh=mesh, in_specs=in_specs, out_specs=out_specs, check_vma=False)
```

```python
import functools
import itertools

import jax
import jax.numpy as jnp
from jax import lax
from jax.experimental import pallas as pl
from jax.experimental.pallas import tpu as pltpu
from jax.sharding import PartitionSpec as P


PROJ_CHANNELS = 32
CZ = 128
H = 4
DH = 32
R_DEV = 8
LANES = 128
PACK = LANES // PROJ_CHANNELS
WINDOW = R_DEV * PROJ_CHANNELS
SPAN = WINDOW + LANES


epsilon = 1e-05
VMEM = pl.BlockSpec(memory_space=pltpu.VMEM)
SMEM = pl.BlockSpec(memory_space=pltpu.SMEM)
ANY = pl.BlockSpec(memory_space=pltpu.HBM)
BF = jnp.bfloat16
F32 = jnp.float32


def call(kernel, outs, specs, scratch=(), flops=0, limit=8, aliases=None):
    return pl.pallas_call(
        kernel,
        out_shape=outs,
        in_specs=specs,
        out_specs=[
            SMEM if getattr(o, "memory_space", None) == pltpu.SMEM else VMEM for o in outs
        ],
        scratch_shapes=list(scratch),
        input_output_aliases=aliases or {},
        compiler_params=pltpu.CompilerParams(vmem_limit_bytes=limit << 20),
        cost_estimate=pl.CostEstimate(
            flops=flops, bytes_accessed=1 << 20, transcendentals=0
        ),
    )


INNER, FAR = 16, 32


def near_price(mask):
    one, inner, far = (jnp.right_shift(mask, n) & 1 for n in (1, 4, 5))
    return one * 5 + inner * 6 + far * 100


def swap_price(mask):
    one, two, three = (jnp.right_shift(mask, n) & 1 for n in (1, 2, 3))
    return one * 5 + two * 12 + three * 10


def front_kernel(adaptive, chip_tokens, left_ref, starts_ref, kept_ref, table_ref, need_ref, raw_ref, sem):
    half = kept_ref.shape[0]
    core = lax.axis_index("res") % 2
    kept_at = pl.multiple_of(core * half, half)
    copies = [
        pltpu.make_async_copy(starts_ref, raw_ref, sem.at[0]),
        pltpu.make_async_copy(left_ref.at[pl.ds(kept_at, half)], kept_ref, sem.at[1]),
    ]
    for copy in copies:
        copy.start()
    copies[0].wait()
    groups = starts_ref.shape[0]
    need_ref[0] = 0
    for g in range(groups):
        table_ref[g] = g
    if adaptive:
        starts = [raw_ref[g] for g in range(groups)]
        reach = []
        for start in starts:
            ends = [start // chip_tokens, (start + (R_DEV - 1)) // chip_tokens]
            reach.append([])
            for h in range(groups):
                bits = 0
                for end in ends:
                    step = jnp.abs(h - end)
                    swap_bits = jnp.bitwise_xor(end, h)
                    bits |= jnp.left_shift(1, swap_bits)
                    bits |= jnp.where((swap_bits == 3) & (step == 1), INNER, 0)
                    bits |= jnp.where(step > 1, FAR, 0)
                reach[-1].append(bits)
        best = cost = homes = None
        for order in itertools.permutations(range(groups)):
            mask = functools.reduce(
                jnp.bitwise_or, [reach[w][h] for h, w in enumerate(order)]
            )
            price = jnp.minimum(near_price(mask), swap_price(mask))
            packed = jnp.int32(sum(w << (4 * h) for h, w in enumerate(order)))
            if best is None:
                best, cost, homes = mask, price, packed
            else:
                better = price < cost
                best = jnp.where(better, mask, best)
                homes = jnp.where(better, packed, homes)
                cost = jnp.where(better, price, cost)
        inner = (best & INNER) > 0
        near = inner & (near_price(best) <= swap_price(best))
        one = jnp.right_shift(best, 1) & 1
        need_ref[0] = jnp.where(near, 8 + one, jnp.right_shift(best, 1) & 7)
        for h in range(groups):
            table_ref[h] = jnp.right_shift(homes, 4 * h) & 15
    for g in range(groups):
        table_ref[groups + g] = raw_ref[table_ref[g]]
    for copy in copies[1:]:
        copy.wait()


def prep_kernel(*refs):
    sources, outs, scratch = refs[:8], refs[8:15], refs[15:]
    wbd_ref, bias_ref, swapped_ref = outs[:3]
    w_ref, tri_ref, chain_ref, off_ref, sem = scratch
    targets = [w_ref, tri_ref, chain_ref, off_ref, *outs[3:]]
    copies = [
        pltpu.make_async_copy(a, b, sem.at[n])
        for n, (a, b) in enumerate(zip(sources, targets))
    ]
    for copy in copies:
        copy.start()
    wbd_ref[...] = jnp.zeros_like(wbd_ref)
    for copy in copies:
        copy.wait()
    for c in range(PROJ_CHANNELS):
        block = w_ref[c * PROJ_CHANNELS : (c + 1) * PROJ_CHANNELS, :]
        for part in range(2):
            for j in range(PACK // 2):
                row = (c // 2) * LANES + (c % 2 ^ part) * (LANES // 2) + j * PROJ_CHANNELS
                wbd_ref[part, row : row + PROJ_CHANNELS, j * CZ : (j + 1) * CZ] = block
    right_ref = outs[3]
    for n in range(right_ref.shape[1] // LANES):
        cols = slice(n * LANES, (n + 1) * LANES)
        block = right_ref[:, cols]
        swapped_ref[:, cols] = jnp.concatenate(
            [block[:, LANES // 2 :], block[:, : LANES // 2]], axis=1
        )
    tokens, keys = tri_ref.shape[1:]
    first = lax.axis_index("res") * tokens
    chain = jnp.broadcast_to(chain_ref[...], (tokens, keys))
    rows = lax.broadcasted_iota(jnp.int32, (tokens, keys), 0)
    cols = lax.broadcasted_iota(jnp.int32, (tokens, keys), 1)
    own = jnp.sum(jnp.where(cols == rows + first, chain, 0), axis=1, keepdims=True)
    differ = (chain != own).astype(F32)
    for h in range(H):
        bias_ref[h * tokens : (h + 1) * tokens, :] = (
            tri_ref[h].astype(F32) + off_ref[h] * differ
        )


def select_kernel(table, own_ref, recv_ref, *refs):
    outs, chip_ref = refs[:-1], refs[-1]
    chips = len(outs)
    size, half = outs[0].shape
    width = own_ref.shape[1]
    res = lax.axis_index("res")
    core = res % 2
    z = res // 2
    own_at = pl.multiple_of(core * width, LANES)
    recv_at = pl.multiple_of((1 - core) * width, LANES)
    chip_ref[:, pl.ds(own_at, width)] = own_ref[...]
    chip_ref[:, pl.ds(recv_at, width)] = recv_ref[pl.ds(pl.multiple_of(core * half, half), half), :]
    m = lax.broadcasted_iota(jnp.int32, (size, SPAN), 0)
    lane = lax.broadcasted_iota(jnp.int32, (size, SPAN), 1)
    half_count = PROJ_CHANNELS // 2
    split = WINDOW // size
    groups = chips // split
    for k in range(chips):
        at = jnp.bitwise_xor(z, k)
        place = at % split * (size // R_DEV) + m // R_DEV
        channel = place % half_count * 2 + place // half_count
        delta = lane - (m % R_DEV) * PROJ_CHANNELS - channel
        start = table[groups + at // split] * PROJ_CHANNELS - z * (2 * width)
        base = jnp.clip(start, 0, 2 * width - SPAN) // LANES * LANES
        base = pl.multiple_of(base, LANES)
        pick = (delta == start - base).astype(F32).astype(BF)
        outs[k][...] = lax.dot_general(
            pick,
            chip_ref[:, pl.ds(base, SPAN)],
            (((1,), (1,)), ((), ())),
            preferred_element_type=F32,
        ).astype(BF)


def outer_kernel(chips, table, *refs):
    mine, theirs = refs[:chips], refs[chips : 2 * chips]
    b_ref, swapped_ref, wbd_ref, *outs = refs[2 * chips : -4]
    at_ref, low_ref, high_ref, acc_ref = refs[-4:]
    size, half = mine[0].shape
    groups = len(outs)
    part_rows = WINDOW // 2
    z = lax.axis_index("res") // 2
    core = lax.axis_index("res") % 2
    mine_at = pl.multiple_of(core * half, LANES)
    theirs_at = pl.multiple_of((1 - core) * half, LANES)
    split = WINDOW // size
    for k in range(chips):
        at = jnp.bitwise_xor(z, k)
        window = table[at // split]
        for n in range(size // part_rows):
            parity = at % split * (size // part_rows) + n
            row = pl.multiple_of((parity * groups + window) * part_rows, part_rows)
            rows = slice(n * part_rows, (n + 1) * part_rows)
            at_ref[pl.ds(row, part_rows), pl.ds(mine_at, half)] = mine[k][rows, :]
            at_ref[pl.ds(row, part_rows), pl.ds(theirs_at, half)] = theirs[k][rows, :]
    width = b_ref.shape[1]
    rows = groups * R_DEV
    pairs = PROJ_CHANNELS // 2
    below = lax.broadcasted_iota(jnp.int32, (rows, LANES), 1) < LANES // 2
    for n in range(width // (2 * LANES)):
        cols = slice(n * 2 * LANES, (n + 1) * 2 * LANES)
        shape = (groups, pairs, R_DEV, 2 * LANES)
        middle = groups * part_rows
        even = jnp.dot(at_ref[:middle, :], b_ref[:, cols], preferred_element_type=F32)
        odd = jnp.dot(at_ref[middle:, :], swapped_ref[:, cols], preferred_element_type=F32)
        even, odd = even.reshape(shape), odd.reshape(shape)
        for c in range(pairs):
            for q in range(2):
                lanes = slice(q * LANES, (q + 1) * LANES)
                x = even[:, c, :, lanes].reshape(rows, LANES)
                y = odd[:, c, :, lanes].reshape(rows, LANES)
                to = slice((2 * n + q) * rows, (2 * n + q + 1) * rows)
                low_ref[to, c * LANES : (c + 1) * LANES] = jnp.where(below, x, y).astype(BF)
                high_ref[to, c * LANES : (c + 1) * LANES] = jnp.where(below, y, x).astype(BF)
    chunks = width // LANES
    wide = PACK * CZ // 2
    for n, ref in enumerate((low_ref, high_ref)):
        acc = jnp.dot(ref[...], wbd_ref[n], preferred_element_type=F32)
        acc_ref[:, :, :, n * wide : (n + 1) * wide] = acc.reshape(chunks, groups, R_DEV, wide)
    for k in range(groups):
        g = jnp.bitwise_xor(lax.axis_index("depth"), k)
        block = acc_ref[:, g]
        block = jnp.stack(
            [block[:, :, j * CZ : (j + 1) * CZ] for j in range(PACK)], axis=1
        )
        outs[k][...] = block.reshape(chunks * PACK * R_DEV, CZ).astype(BF)


def norm_kernel(scale, *refs):
    parts = refs[:-4]
    bias_ref, pair_ref, normed_ref, sum_ref = refs[-4:]
    total = parts[0][...].astype(F32)
    for p in parts[1:]:
        total = total + p[...].astype(F32)
    sum_ref[...] = total * scale + bias_ref[...]
    tokens = pair_ref.shape[1]
    for u in range(R_DEV):
        pair = sum_ref[pl.ds(u, tokens, stride=R_DEV), :].astype(BF)
        pair_ref[u] = pair
        values = pair.astype(F32)
        centred = values - jnp.mean(values, axis=-1, keepdims=True)
        variance = jnp.mean(centred * centred, axis=-1, keepdims=True)
        normed_ref[u] = (centred * lax.rsqrt(variance + epsilon)).astype(BF)


def query_kernel(normed_ref, w_ref, pair_ref, q_ref, gate_ref, strip_ref):
    strip_ref[...] = pair_ref[...]
    rows = R_DEV * normed_ref.shape[1]
    x = normed_ref[...].reshape(rows, CZ)
    q_ref[...] = jnp.dot(x, w_ref[:, :CZ], preferred_element_type=F32).astype(BF)
    g = jnp.dot(x, w_ref[:, 3 * CZ :], preferred_element_type=F32).astype(BF)
    gate_ref[...] = jax.nn.sigmoid(g.astype(F32))


def near_kernel(chips, *refs):
    near, w_ref, kv_ref = refs[:chips], refs[chips], refs[chips + 1]
    fill(near, w_ref, kv_ref, lax.axis_index("res") % 2)


def fill(pieces, w_ref, kv_ref, core):
    tokens = pieces[0].shape[1]
    z = lax.axis_index("res") // 2
    for k, piece in enumerate(pieces):
        at = (jnp.bitwise_xor(z, k) * 2 + core) * tokens
        kv = jnp.dot(
            piece[...].reshape(R_DEV * tokens, CZ),
            w_ref[:, CZ : 3 * CZ],
            preferred_element_type=F32,
        )
        kv_ref[:, pl.ds(pl.multiple_of(at, tokens), tokens), :] = kv.astype(BF).reshape(
            R_DEV, tokens, 2 * CZ
        )


def attend_kernel(chips, *refs):
    far = refs[:chips]
    _, q_ref, gate_ref, w_ref, wo_ref, bias_ref, out_ref, kv_ref = refs[chips:-2]
    scores_ref, gated_ref = refs[-2:]
    tokens = far[0].shape[1]
    fill(far, w_ref, kv_ref, 1 - lax.axis_index("res") % 2)
    scale = DH ** (-0.5)
    lane_head = lax.broadcasted_iota(jnp.int32, (tokens, CZ), 1) // DH
    for u in range(R_DEV):
        q = q_ref[u * tokens : (u + 1) * tokens, :]
        spread = jnp.concatenate(
            [jnp.where(lane_head == h, q, jnp.zeros_like(q)) for h in range(H)], axis=0
        )
        scores = lax.dot_general(
            spread, kv_ref[u, :, :CZ], (((1,), (1,)), ((), ())), preferred_element_type=F32
        )
        scores_ref[u] = scores * scale + bias_ref[...]
    for u in range(R_DEV):
        scores = scores_ref[u]
        weights = jnp.exp(scores - jnp.max(scores, axis=-1, keepdims=True))
        denom = jnp.sum(weights, axis=-1, keepdims=True)
        value = jnp.dot(
            weights.astype(BF), kv_ref[u, :, CZ:], preferred_element_type=F32
        )
        value = value / denom
        attended = jnp.zeros((tokens, CZ), F32)
        for h in range(H):
            attended = jnp.where(
                lane_head == h, value[h * tokens : (h + 1) * tokens, :], attended
            )
        gated_ref[u * tokens : (u + 1) * tokens, :] = (
            gate_ref[u * tokens : (u + 1) * tokens, :] * attended
        ).astype(BF)
    out = jnp.dot(gated_ref[...], wo_ref[...], preferred_element_type=F32)
    out_ref[...] = out.astype(BF).reshape(R_DEV, tokens, CZ)


def in_hbm(*arrays):
    return [pltpu.with_memory_space_constraint(a, pltpu.HBM) for a in arrays]


def swap(x, axis, mask):
    n = lax.axis_size(axis)
    return lax.ppermute(x, axis, [(i, i ^ mask) for i in range(n)])


def body(
    alignment_left,
    alignment_right,
    window_starts,
    outer_product_weight,
    outer_product_bias,
    query_key_value_gate_weight,
    output_weight,
    triangle_pair_bias,
    residue_chain,
    interchain_offset,
):
    depth_count = lax.axis_size("depth")
    res_count = lax.axis_size("res")
    groups = window_starts.shape[0]
    chips = res_count // 2
    size = groups * WINDOW // chips
    assert groups == depth_count and WINDOW % size == 0
    seqs, width = alignment_left.shape
    half = seqs // 2
    tokens = width // PROJ_CHANNELS
    keys = residue_chain.shape[0]
    rows = groups * R_DEV

    adaptive = chips == groups == 4
    kept, table, need = call(
        functools.partial(front_kernel, adaptive, 2 * tokens),
        [
            pltpu.VMEM((half, width), BF),
            pltpu.SMEM((2 * groups,), jnp.int32),
            pltpu.SMEM((1,), jnp.int32),
        ],
        [ANY, ANY],
        [pltpu.SMEM(window_starts.shape, jnp.int32), pltpu.SemaphoreType.DMA((2,))],
    )(*in_hbm(alignment_left, window_starts))
    recv = swap(alignment_left, "res", 1)

    wbd, bias, swapped, right, qkvg, wo, shift = call(
        prep_kernel,
        [
            pltpu.VMEM((2, PROJ_CHANNELS * LANES // 2, PACK * CZ // 2), BF),
            pltpu.VMEM((H * tokens, keys), F32),
            pltpu.VMEM(alignment_right.shape, BF),
            pltpu.VMEM(alignment_right.shape, BF),
            pltpu.VMEM(query_key_value_gate_weight.shape, BF),
            pltpu.VMEM(output_weight.shape, BF),
            pltpu.VMEM((1, CZ), F32),
        ],
        [ANY] * 8,
        [
            pltpu.VMEM(outer_product_weight.shape, BF),
            pltpu.VMEM(triangle_pair_bias.shape, BF),
            pltpu.VMEM((1, keys), jnp.int32),
            pltpu.SMEM((H,), F32),
            pltpu.SemaphoreType.DMA((8,)),
        ],
        flops=1 << 28,
    )(
        *in_hbm(
            outer_product_weight,
            triangle_pair_bias,
            residue_chain[None, :],
            interchain_offset,
            alignment_right,
            query_key_value_gate_weight,
            output_weight,
            outer_product_bias[None, :],
        )
    )

    picked = call(
        select_kernel,
        [pltpu.VMEM((size, half), BF)] * chips,
        [SMEM, VMEM, VMEM],
        [pltpu.VMEM((half, 2 * width), BF)],
        flops=1 << 28,
    )(table, kept, recv)

    def collect(wanted, *picked):
        return functools.reduce(
            jnp.add,
            [picked[0]] + [swap(picked[k], "res", 2 * k) for k in wanted],
        )

    def collect_near(one, *picked):
        inner = [r for r in range(res_count) if abs(r // 2 - (r ^ 6) // 2) == 1]
        pairs = [(r, r ^ 6 if r in inner else r ^ 1) for r in range(res_count)]
        moved = [picked[0], lax.ppermute(picked[3], "res", pairs)]
        if one:
            moved.append(swap(picked[1], "res", 2))
        return functools.reduce(jnp.add, moved)

    every = range(1, chips)
    if adaptive:
        subsets = [
            [k for k in every if bits >> (k - 1) & 1] for bits in range(1 << len(every))
        ]
        branches = [functools.partial(collect, wanted) for wanted in subsets]
        branches += [functools.partial(collect_near, one) for one in (False, True)]
        piece = lax.switch(need[0], branches, *picked)
    else:
        piece = collect(every, *picked)
    mine = [piece] + [swap(piece, "res", 2 * k) for k in range(1, chips)]
    theirs = [swap(m, "res", 1) for m in mine]

    partial = call(
        functools.partial(outer_kernel, chips),
        [pltpu.VMEM((R_DEV * tokens, CZ), BF)] * groups,
        [SMEM] + [VMEM] * (2 * chips + 3),
        [
            pltpu.VMEM((groups * WINDOW, seqs), BF),
            pltpu.VMEM((rows * width // LANES, PROJ_CHANNELS * LANES // 2), BF),
            pltpu.VMEM((rows * width // LANES, PROJ_CHANNELS * LANES // 2), BF),
            pltpu.VMEM((width // LANES, groups, R_DEV, PACK * CZ), F32),
        ],
        flops=1 << 31,
        limit=32,
    )(table, *mine, *theirs, right, swapped, wbd)
    parts = [partial[0]] + [swap(partial[k], "depth", k) for k in range(1, groups)]

    pair, normed = call(
        functools.partial(norm_kernel, 1.0 / (seqs * depth_count)),
        [pltpu.VMEM((R_DEV, tokens, CZ), BF)] * 2,
        [VMEM] * (groups + 1),
        [pltpu.VMEM((R_DEV * tokens, CZ), F32)],
        flops=1 << 24,
    )(*parts, shift)

    near = [normed] + [swap(normed, "res", 2 * k) for k in range(1, chips)]
    far = [swap(n, "res", 1) for n in near]
    queries, gate, pair_strip = call(
        query_kernel,
        [
            pltpu.VMEM((R_DEV * tokens, CZ), BF),
            pltpu.VMEM((R_DEV * tokens, CZ), F32),
            jax.ShapeDtypeStruct((R_DEV, tokens, CZ), BF),
        ],
        [VMEM] * 3,
        flops=1 << 27,
    )(normed, qkvg, pair)
    kv = pltpu.VMEM((R_DEV, keys, 2 * CZ), BF)
    (half_kv,) = call(
        functools.partial(near_kernel, chips), [kv], [VMEM] * (chips + 1), flops=1 << 28
    )(*near, qkvg)
    update, _ = call(
        functools.partial(attend_kernel, chips),
        [jax.ShapeDtypeStruct((R_DEV, tokens, CZ), BF), kv],
        [VMEM] * (chips + 6),
        [
            pltpu.VMEM((R_DEV, H * tokens, keys), F32),
            pltpu.VMEM((R_DEV * tokens, CZ), BF),
        ],
        flops=1 << 29,
        limit=24,
        aliases={chips: 1},
    )(*far, half_kv, queries, gate, qkvg, wo, bias)
    return (pair_strip, update)


def solution(mesh):
    in_specs = (
        P("depth", "res"),
        P("depth", "res"),
        P(),
        P(),
        P(),
        P(),
        P(),
        P(None, "res", None),
        P(),
        P(),
    )
    out_specs = (P("depth", "res", None), P("depth", "res", None))
    return jax.shard_map(body, mesh=mesh, in_specs=in_specs, out_specs=out_specs, check_vma=False)
```

```python
import functools
import itertools

import jax
import jax.numpy as jnp
from jax import lax
from jax.experimental import pallas as pl
from jax.experimental.pallas import tpu as pltpu
from jax.sharding import PartitionSpec as P


PROJ_CHANNELS = 32
CZ = 128
H = 4
DH = 32
R_DEV = 8
LANES = 128
PACK = LANES // PROJ_CHANNELS
WINDOW = R_DEV * PROJ_CHANNELS
SPAN = WINDOW + LANES


epsilon = 1e-05
VMEM = pl.BlockSpec(memory_space=pltpu.VMEM)
SMEM = pl.BlockSpec(memory_space=pltpu.SMEM)
ANY = pl.BlockSpec(memory_space=pltpu.HBM)
BF = jnp.bfloat16
F32 = jnp.float32


def call(kernel, outs, specs, scratch=(), flops=0, limit=8, aliases=None):
    return pl.pallas_call(
        kernel,
        out_shape=outs,
        in_specs=specs,
        out_specs=[
            SMEM if getattr(o, "memory_space", None) == pltpu.SMEM else VMEM for o in outs
        ],
        scratch_shapes=list(scratch),
        input_output_aliases=aliases or {},
        compiler_params=pltpu.CompilerParams(vmem_limit_bytes=limit << 20),
        cost_estimate=pl.CostEstimate(
            flops=flops, bytes_accessed=1 << 20, transcendentals=0
        ),
    )


INNER, FAR = 16, 32


def near_price(mask):
    one, inner, far = (jnp.right_shift(mask, n) & 1 for n in (1, 4, 5))
    return one * 5 + inner * 6 + far * 100


def swap_price(mask):
    one, two, three = (jnp.right_shift(mask, n) & 1 for n in (1, 2, 3))
    return one * 5 + two * 12 + three * 10


def front_kernel(adaptive, chip_tokens, left_ref, starts_ref, kept_ref, table_ref, need_ref, raw_ref, sem):
    half = kept_ref.shape[0]
    core = lax.axis_index("res") % 2
    kept_at = pl.multiple_of(core * half, half)
    copies = [
        pltpu.make_async_copy(starts_ref, raw_ref, sem.at[0]),
        pltpu.make_async_copy(left_ref.at[pl.ds(kept_at, half)], kept_ref, sem.at[1]),
    ]
    for copy in copies:
        copy.start()
    copies[0].wait()
    groups = starts_ref.shape[0]
    need_ref[0] = 0
    for g in range(groups):
        table_ref[g] = g
    if adaptive:
        starts = [raw_ref[g] for g in range(groups)]
        reach = []
        for start in starts:
            ends = [start // chip_tokens, (start + (R_DEV - 1)) // chip_tokens]
            reach.append([])
            for h in range(groups):
                bits = 0
                for end in ends:
                    step = jnp.abs(h - end)
                    swap_bits = jnp.bitwise_xor(end, h)
                    bits |= jnp.left_shift(1, swap_bits)
                    bits |= jnp.where((swap_bits == 3) & (step == 1), INNER, 0)
                    bits |= jnp.where(step > 1, FAR, 0)
                reach[-1].append(bits)
        best = cost = homes = None
        for order in itertools.permutations(range(groups)):
            mask = functools.reduce(
                jnp.bitwise_or, [reach[w][h] for h, w in enumerate(order)]
            )
            price = jnp.minimum(near_price(mask), swap_price(mask))
            packed = jnp.int32(sum(w << (4 * h) for h, w in enumerate(order)))
            if best is None:
                best, cost, homes = mask, price, packed
            else:
                better = price < cost
                best = jnp.where(better, mask, best)
                homes = jnp.where(better, packed, homes)
                cost = jnp.where(better, price, cost)
        inner = (best & INNER) > 0
        near = inner & (near_price(best) <= swap_price(best))
        one = jnp.right_shift(best, 1) & 1
        need_ref[0] = jnp.where(near, 8 + one, jnp.right_shift(best, 1) & 7)
        for h in range(groups):
            table_ref[h] = jnp.right_shift(homes, 4 * h) & 15
    for g in range(groups):
        table_ref[groups + g] = raw_ref[table_ref[g]]
    for copy in copies[1:]:
        copy.wait()


def prep_kernel(*refs):
    sources, outs, scratch = refs[:8], refs[8:15], refs[15:]
    wbd_ref, bias_ref, swapped_ref = outs[:3]
    w_ref, tri_ref, chain_ref, off_ref, sem = scratch
    targets = [w_ref, tri_ref, chain_ref, off_ref, *outs[3:]]
    copies = [
        pltpu.make_async_copy(a, b, sem.at[n])
        for n, (a, b) in enumerate(zip(sources, targets))
    ]
    for copy in copies:
        copy.start()
    wbd_ref[...] = jnp.zeros_like(wbd_ref)
    for copy in copies:
        copy.wait()
    for c in range(PROJ_CHANNELS):
        block = w_ref[c * PROJ_CHANNELS : (c + 1) * PROJ_CHANNELS, :]
        for part in range(2):
            for j in range(PACK // 2):
                row = (c // 2) * LANES + (c % 2 ^ part) * (LANES // 2) + j * PROJ_CHANNELS
                wbd_ref[part, row : row + PROJ_CHANNELS, j * CZ : (j + 1) * CZ] = block
    right_ref = outs[3]
    for n in range(right_ref.shape[1] // LANES):
        cols = slice(n * LANES, (n + 1) * LANES)
        block = right_ref[:, cols]
        swapped_ref[:, cols] = jnp.concatenate(
            [block[:, LANES // 2 :], block[:, : LANES // 2]], axis=1
        )
    tokens, keys = tri_ref.shape[1:]
    first = lax.axis_index("res") * tokens
    chain = jnp.broadcast_to(chain_ref[...], (tokens, keys))
    rows = lax.broadcasted_iota(jnp.int32, (tokens, keys), 0)
    cols = lax.broadcasted_iota(jnp.int32, (tokens, keys), 1)
    own = jnp.sum(jnp.where(cols == rows + first, chain, 0), axis=1, keepdims=True)
    differ = (chain != own).astype(F32)
    for h in range(H):
        bias_ref[h * tokens : (h + 1) * tokens, :] = (
            tri_ref[h].astype(F32) + off_ref[h] * differ
        )


def select_kernel(table, own_ref, recv_ref, *refs):
    outs, chip_ref = refs[:-1], refs[-1]
    chips = len(outs)
    size, half = outs[0].shape
    width = own_ref.shape[1]
    res = lax.axis_index("res")
    core = res % 2
    z = res // 2
    own_at = pl.multiple_of(core * width, LANES)
    recv_at = pl.multiple_of((1 - core) * width, LANES)
    chip_ref[:, pl.ds(own_at, width)] = own_ref[...]
    chip_ref[:, pl.ds(recv_at, width)] = recv_ref[pl.ds(pl.multiple_of(core * half, half), half), :]
    m = lax.broadcasted_iota(jnp.int32, (size, SPAN), 0)
    lane = lax.broadcasted_iota(jnp.int32, (size, SPAN), 1)
    half_count = PROJ_CHANNELS // 2
    split = WINDOW // size
    groups = chips // split
    for k in range(chips):
        at = jnp.bitwise_xor(z, k)
        place = at % split * (size // R_DEV) + m // R_DEV
        channel = place % half_count * 2 + place // half_count
        delta = lane - (m % R_DEV) * PROJ_CHANNELS - channel
        start = table[groups + at // split] * PROJ_CHANNELS - z * (2 * width)
        base = jnp.clip(start, 0, 2 * width - SPAN) // LANES * LANES
        base = pl.multiple_of(base, LANES)
        pick = (delta == start - base).astype(F32).astype(BF)
        outs[k][...] = lax.dot_general(
            pick,
            chip_ref[:, pl.ds(base, SPAN)],
            (((1,), (1,)), ((), ())),
            preferred_element_type=F32,
        ).astype(BF)


def outer_kernel(chips, table, *refs):
    mine, theirs = refs[:chips], refs[chips : 2 * chips]
    b_ref, swapped_ref, wbd_ref, *outs = refs[2 * chips : -4]
    at_ref, low_ref, high_ref, acc_ref = refs[-4:]
    size, half = mine[0].shape
    groups = len(outs)
    part_rows = WINDOW // 2
    z = lax.axis_index("res") // 2
    core = lax.axis_index("res") % 2
    mine_at = pl.multiple_of(core * half, LANES)
    theirs_at = pl.multiple_of((1 - core) * half, LANES)
    split = WINDOW // size
    for k in range(chips):
        at = jnp.bitwise_xor(z, k)
        window = table[at // split]
        for n in range(size // part_rows):
            parity = at % split * (size // part_rows) + n
            row = pl.multiple_of((parity * groups + window) * part_rows, part_rows)
            rows = slice(n * part_rows, (n + 1) * part_rows)
            at_ref[pl.ds(row, part_rows), pl.ds(mine_at, half)] = mine[k][rows, :]
            at_ref[pl.ds(row, part_rows), pl.ds(theirs_at, half)] = theirs[k][rows, :]
    width = b_ref.shape[1]
    rows = groups * R_DEV
    pairs = PROJ_CHANNELS // 2
    below = lax.broadcasted_iota(jnp.int32, (rows, LANES), 1) < LANES // 2
    for n in range(width // (2 * LANES)):
        cols = slice(n * 2 * LANES, (n + 1) * 2 * LANES)
        shape = (groups, pairs, R_DEV, 2 * LANES)
        middle = groups * part_rows
        even = jnp.dot(at_ref[:middle, :], b_ref[:, cols], preferred_element_type=F32)
        odd = jnp.dot(at_ref[middle:, :], swapped_ref[:, cols], preferred_element_type=F32)
        even, odd = even.reshape(shape), odd.reshape(shape)
        for c in range(pairs):
            for q in range(2):
                lanes = slice(q * LANES, (q + 1) * LANES)
                x = even[:, c, :, lanes].reshape(rows, LANES)
                y = odd[:, c, :, lanes].reshape(rows, LANES)
                to = slice((2 * n + q) * rows, (2 * n + q + 1) * rows)
                low_ref[to, c * LANES : (c + 1) * LANES] = jnp.where(below, x, y).astype(BF)
                high_ref[to, c * LANES : (c + 1) * LANES] = jnp.where(below, y, x).astype(BF)
    chunks = width // LANES
    wide = PACK * CZ // 2
    for n, ref in enumerate((low_ref, high_ref)):
        acc = jnp.dot(ref[...], wbd_ref[n], preferred_element_type=F32)
        acc_ref[:, :, :, n * wide : (n + 1) * wide] = acc.reshape(chunks, groups, R_DEV, wide)
    for k in range(groups):
        g = jnp.bitwise_xor(lax.axis_index("depth"), k)
        block = acc_ref[:, g]
        block = jnp.stack(
            [block[:, :, j * CZ : (j + 1) * CZ] for j in range(PACK)], axis=1
        )
        outs[k][...] = block.reshape(chunks * PACK * R_DEV, CZ).astype(BF)


def norm_kernel(scale, *refs):
    parts = refs[:-4]
    bias_ref, pair_ref, normed_ref, sum_ref = refs[-4:]
    total = parts[0][...].astype(F32)
    for p in parts[1:]:
        total = total + p[...].astype(F32)
    sum_ref[...] = total * scale + bias_ref[...]
    tokens = pair_ref.shape[1]
    for u in range(R_DEV):
        pair = sum_ref[pl.ds(u, tokens, stride=R_DEV), :].astype(BF)
        pair_ref[u] = pair
        values = pair.astype(F32)
        centred = values - jnp.mean(values, axis=-1, keepdims=True)
        variance = jnp.mean(centred * centred, axis=-1, keepdims=True)
        normed_ref[u] = (centred * lax.rsqrt(variance + epsilon)).astype(BF)


def query_kernel(normed_ref, w_ref, pair_ref, q_ref, gate_ref, strip_ref):
    strip_ref[...] = pair_ref[...]
    rows = R_DEV * normed_ref.shape[1]
    x = normed_ref[...].reshape(rows, CZ)
    q_ref[...] = jnp.dot(x, w_ref[:, :CZ], preferred_element_type=F32).astype(BF)
    g = jnp.dot(x, w_ref[:, 3 * CZ :], preferred_element_type=F32).astype(BF)
    gate_ref[...] = jax.nn.sigmoid(g.astype(F32))


def near_kernel(chips, *refs):
    near, partner, w_ref, kv_ref = refs[:chips], *refs[chips:]
    core = lax.axis_index("res") % 2
    fill(near, w_ref, kv_ref, core, 0)
    fill([partner], w_ref, kv_ref, 1 - core, 0)


def fill(pieces, w_ref, kv_ref, core, first):
    tokens = pieces[0].shape[1]
    z = lax.axis_index("res") // 2
    for k, piece in enumerate(pieces, first):
        at = (jnp.bitwise_xor(z, k) * 2 + core) * tokens
        kv = jnp.dot(
            piece[...].reshape(R_DEV * tokens, CZ),
            w_ref[:, CZ : 3 * CZ],
            preferred_element_type=F32,
        )
        kv_ref[:, pl.ds(pl.multiple_of(at, tokens), tokens), :] = kv.astype(BF).reshape(
            R_DEV, tokens, 2 * CZ
        )


def attend_kernel(chips, *refs):
    far = refs[: chips - 1]
    _, q_ref, gate_ref, w_ref, wo_ref, bias_ref, out_ref, kv_ref = refs[chips - 1 : -2]
    scores_ref, gated_ref = refs[-2:]
    tokens = far[0].shape[1]
    fill(far, w_ref, kv_ref, 1 - lax.axis_index("res") % 2, 1)
    scale = DH ** (-0.5)
    lane_head = lax.broadcasted_iota(jnp.int32, (tokens, CZ), 1) // DH
    for u in range(R_DEV):
        q = q_ref[u * tokens : (u + 1) * tokens, :]
        spread = jnp.concatenate(
            [jnp.where(lane_head == h, q, jnp.zeros_like(q)) for h in range(H)], axis=0
        )
        scores = lax.dot_general(
            spread, kv_ref[u, :, :CZ], (((1,), (1,)), ((), ())), preferred_element_type=F32
        )
        scores_ref[u] = scores * scale + bias_ref[...]
    for u in range(R_DEV):
        scores = scores_ref[u]
        weights = jnp.exp(scores - jnp.max(scores, axis=-1, keepdims=True))
        denom = jnp.sum(weights, axis=-1, keepdims=True)
        value = jnp.dot(
            weights.astype(BF), kv_ref[u, :, CZ:], preferred_element_type=F32
        )
        value = value / denom
        attended = jnp.zeros((tokens, CZ), F32)
        for h in range(H):
            attended = jnp.where(
                lane_head == h, value[h * tokens : (h + 1) * tokens, :], attended
            )
        gated_ref[u * tokens : (u + 1) * tokens, :] = (
            gate_ref[u * tokens : (u + 1) * tokens, :] * attended
        ).astype(BF)
    out = jnp.dot(gated_ref[...], wo_ref[...], preferred_element_type=F32)
    out_ref[...] = out.astype(BF).reshape(R_DEV, tokens, CZ)


def in_hbm(*arrays):
    return [pltpu.with_memory_space_constraint(a, pltpu.HBM) for a in arrays]


def swap(x, axis, mask):
    n = lax.axis_size(axis)
    return lax.ppermute(x, axis, [(i, i ^ mask) for i in range(n)])


def body(
    alignment_left,
    alignment_right,
    window_starts,
    outer_product_weight,
    outer_product_bias,
    query_key_value_gate_weight,
    output_weight,
    triangle_pair_bias,
    residue_chain,
    interchain_offset,
):
    depth_count = lax.axis_size("depth")
    res_count = lax.axis_size("res")
    groups = window_starts.shape[0]
    chips = res_count // 2
    size = groups * WINDOW // chips
    assert groups == depth_count and WINDOW % size == 0
    seqs, width = alignment_left.shape
    half = seqs // 2
    tokens = width // PROJ_CHANNELS
    keys = residue_chain.shape[0]
    rows = groups * R_DEV

    adaptive = chips == groups == 4
    kept, table, need = call(
        functools.partial(front_kernel, adaptive, 2 * tokens),
        [
            pltpu.VMEM((half, width), BF),
            pltpu.SMEM((2 * groups,), jnp.int32),
            pltpu.SMEM((1,), jnp.int32),
        ],
        [ANY, ANY],
        [pltpu.SMEM(window_starts.shape, jnp.int32), pltpu.SemaphoreType.DMA((2,))],
    )(*in_hbm(alignment_left, window_starts))
    recv = swap(alignment_left, "res", 1)

    wbd, bias, swapped, right, qkvg, wo, shift = call(
        prep_kernel,
        [
            pltpu.VMEM((2, PROJ_CHANNELS * LANES // 2, PACK * CZ // 2), BF),
            pltpu.VMEM((H * tokens, keys), F32),
            pltpu.VMEM(alignment_right.shape, BF),
            pltpu.VMEM(alignment_right.shape, BF),
            pltpu.VMEM(query_key_value_gate_weight.shape, BF),
            pltpu.VMEM(output_weight.shape, BF),
            pltpu.VMEM((1, CZ), F32),
        ],
        [ANY] * 8,
        [
            pltpu.VMEM(outer_product_weight.shape, BF),
            pltpu.VMEM(triangle_pair_bias.shape, BF),
            pltpu.VMEM((1, keys), jnp.int32),
            pltpu.SMEM((H,), F32),
            pltpu.SemaphoreType.DMA((8,)),
        ],
        flops=1 << 28,
    )(
        *in_hbm(
            outer_product_weight,
            triangle_pair_bias,
            residue_chain[None, :],
            interchain_offset,
            alignment_right,
            query_key_value_gate_weight,
            output_weight,
            outer_product_bias[None, :],
        )
    )

    picked = call(
        select_kernel,
        [pltpu.VMEM((size, half), BF)] * chips,
        [SMEM, VMEM, VMEM],
        [pltpu.VMEM((half, 2 * width), BF)],
        flops=1 << 28,
    )(table, kept, recv)

    def collect(wanted, *picked):
        return functools.reduce(
            jnp.add,
            [picked[0]] + [swap(picked[k], "res", 2 * k) for k in wanted],
        )

    def collect_near(one, *picked):
        inner = [r for r in range(res_count) if abs(r // 2 - (r ^ 6) // 2) == 1]
        pairs = [(r, r ^ 6 if r in inner else r ^ 1) for r in range(res_count)]
        moved = [picked[0], lax.ppermute(picked[3], "res", pairs)]
        if one:
            moved.append(swap(picked[1], "res", 2))
        return functools.reduce(jnp.add, moved)

    every = range(1, chips)
    if adaptive:
        subsets = [
            [k for k in every if bits >> (k - 1) & 1] for bits in range(1 << len(every))
        ]
        branches = [functools.partial(collect, wanted) for wanted in subsets]
        branches += [functools.partial(collect_near, one) for one in (False, True)]
        piece = lax.switch(need[0], branches, *picked)
    else:
        piece = collect(every, *picked)
    mine = [piece] + [swap(piece, "res", 2 * k) for k in range(1, chips)]
    theirs = [swap(m, "res", 1) for m in mine]

    partial = call(
        functools.partial(outer_kernel, chips),
        [pltpu.VMEM((R_DEV * tokens, CZ), BF)] * groups,
        [SMEM] + [VMEM] * (2 * chips + 3),
        [
            pltpu.VMEM((groups * WINDOW, seqs), BF),
            pltpu.VMEM((rows * width // LANES, PROJ_CHANNELS * LANES // 2), BF),
            pltpu.VMEM((rows * width // LANES, PROJ_CHANNELS * LANES // 2), BF),
            pltpu.VMEM((width // LANES, groups, R_DEV, PACK * CZ), F32),
        ],
        flops=1 << 31,
        limit=32,
    )(table, *mine, *theirs, right, swapped, wbd)
    parts = [partial[0]] + [swap(partial[k], "depth", k) for k in range(1, groups)]

    pair, normed = call(
        functools.partial(norm_kernel, 1.0 / (seqs * depth_count)),
        [pltpu.VMEM((R_DEV, tokens, CZ), BF)] * 2,
        [VMEM] * (groups + 1),
        [pltpu.VMEM((R_DEV * tokens, CZ), F32)],
        flops=1 << 24,
    )(*parts, shift)

    near = [normed] + [swap(normed, "res", 2 * k) for k in range(1, chips)]
    far = [swap(n, "res", 1) for n in near]
    queries, gate, pair_strip = call(
        query_kernel,
        [
            pltpu.VMEM((R_DEV * tokens, CZ), BF),
            pltpu.VMEM((R_DEV * tokens, CZ), F32),
            jax.ShapeDtypeStruct((R_DEV, tokens, CZ), BF),
        ],
        [VMEM] * 3,
        flops=1 << 27,
    )(normed, qkvg, pair)
    kv = pltpu.VMEM((R_DEV, keys, 2 * CZ), BF)
    (half_kv,) = call(
        functools.partial(near_kernel, chips), [kv], [VMEM] * (chips + 2), flops=1 << 28
    )(*near, far[0], qkvg)
    update, _ = call(
        functools.partial(attend_kernel, chips),
        [jax.ShapeDtypeStruct((R_DEV, tokens, CZ), BF), kv],
        [VMEM] * (chips + 5),
        [
            pltpu.VMEM((R_DEV, H * tokens, keys), F32),
            pltpu.VMEM((R_DEV * tokens, CZ), BF),
        ],
        flops=1 << 29,
        limit=24,
        aliases={chips - 1: 1},
    )(*far[1:], half_kv, queries, gate, qkvg, wo, bias)
    return (pair_strip, update)


def solution(mesh):
    in_specs = (
        P("depth", "res"),
        P("depth", "res"),
        P(),
        P(),
        P(),
        P(),
        P(),
        P(None, "res", None),
        P(),
        P(),
    )
    out_specs = (P("depth", "res", None), P("depth", "res", None))
    return jax.shard_map(body, mesh=mesh, in_specs=in_specs, out_specs=out_specs, check_vma=False)
```
